32 devices in a mesh: groups: 2 (over y), tensor: 8 (over z, x), seq: 2 (over core).
Axes of the slice: x: 2, y: 2, z: 4, core: 2. Of those that a mesh axis runs over, the one named last changes fastest.
Arguments:
- stored_hidden: bfloat16 [4, 64, 7168], P(('groups', 'seq'), None, 'tensor'), parts along dimension 0, may hold values from -6 to 6
- w_down_kv: bfloat16 [7168, 576], P('tensor'), may hold values from -0.0625 to 0.0625
- kv_gain: bfloat16 [512], replicated, may hold values from 0.5 to 1.5
- evicted_blocks: int32 [2], P('groups'), parts along dimension 0, may hold values from 0 to 127, as said below
- query_latent: bfloat16 [64, 1536], P(('groups', 'tensor')), parts along dimension 0, may hold values from -6 to 6
- w_up_q: bfloat16 [1536, 24576], P(None, 'tensor'), may hold values from -0.15625 to 0.15625
- w_key_absorb: bfloat16 [128, 128, 512], P('tensor'), may hold values from -0.5 to 0.5
- w_value: bfloat16 [128, 512, 128], P('tensor'), may hold values from -0.25 to 0.25
- query_positions: int32 [64], P('groups'), parts along dimension 0, may hold values from 16384 to 32767
- prefix_lengths: int32 [8], P('groups'), parts along dimension 0, may hold values from 4096 to 16384, as said below
- latent_cache: bfloat16 [32768, 576], P(('groups', 'seq')), parts along dimension 0, may hold values from -500 to 500
Outputs:
- rebuilt: bfloat16 [4, 64, 576], P(('groups', 'seq'), 'tensor'), parts along dimension 0
- attended: bfloat16 [64, 16384], P('groups', 'tensor'), parts along dimension 0
The draws below stay inside these ranges and needn't reach their ends.
There are 2 independent parts, one for each index of `groups`. The reference program is written for one: setup_inputs(seed, part) draws one part's arguments, and reference() takes and returns one part's arrays. A program takes and returns all parts, laid end to end along the dimension named above; an argument that names none is the same for every part. Nothing has to cross between parts.
Inputs may be any that keep to these rules, and one draw needn't show every extreme that they name: `evicted_blocks`: distinct block numbers of the cached prefix. `prefix_lengths`: one request's length is exactly 16384.
All inputs are finite; a program needn't handle non-finite values.
Results may differ from the reference program's by a relative error of at most 0.012.
The reference program's roundings to bfloat16 on the way count: a program that leaves them out, or rounds other values in their place, can miss the bound.
Values may be sent and summed in bfloat16 or wider, within the bound.
A program may use at most 64 MiB of HBM per device.

```python
import jax
import jax.numpy as jnp
from jax import lax

D = 7168
KV_RANK = 512
QL = 1536
H = 128
NOPE = 128
VH = 128
BLK = 128
REQUESTS = 4
E_HALF = 64
EVICTED = 128
S = 16384
Q = 32
C = 576
QK = 192
N_SEQ = 2


def draw_evicted_blocks(key, part):
    block_total = S // BLK
    shuffled = jax.random.permutation(key, block_total)
    chosen = shuffled[:EVICTED // BLK]
    return ((chosen - chosen[0] + block_total - 1) % block_total).astype(jnp.int32)


def draw_prefix_lengths(key, part):
    values_drawn = jax.random.randint(key, (REQUESTS,), S // 4, S + 1)
    picked = jax.random.permutation(jax.random.fold_in(key, 7), REQUESTS)
    return values_drawn.at[picked[0]].set(S).at[picked[1]].set(S // 4).astype(jnp.int32)


def draw_latent_cache(key, part):
    drawn_cache = jax.random.normal(key, (S, C), jnp.float32)
    return drawn_cache.astype(jnp.bfloat16)


def touch_ends(array, own_key, low, top_value):
    longest = array.shape.index(max(array.shape))
    spots = []
    for shift in (0, 1):
        where = [jax.random.randint(jax.random.fold_in(own_key, axis), (), 0, length) for axis, length in enumerate(array.shape)]
        where[longest] = (where[longest] + shift) % array.shape[longest]
        spots.append(tuple(where))
    return array.at[spots[0]].set(low).at[spots[1]].set(top_value)


def spiked(values, own_key, source, target, parts, factor):
    owner, partner = [(jnp.arange(values.shape[axis_at]) // (values.shape[axis_at] // parts)).reshape([-1 if axis == axis_at else 1 for axis in range(values.ndim)]) for axis_at in (source, target)]
    chosen = jax.random.permutation(own_key, parts)[partner]
    strong = (owner == chosen) | (owner == (partner + parts // 2) % parts)
    return jnp.where(strong, factor * values, values)


def levels(stream_key, dims, cuts, low, top_value):
    loudness = 1.0
    for dim, parts in cuts:
        heights = jax.random.uniform(jax.random.fold_in(jax.random.fold_in(stream_key, 6), dim), (parts,), jnp.float32, low / len(cuts), top_value / len(cuts))
        loudness = loudness * jnp.repeat(jnp.exp(heights), dims[dim] // parts).reshape((-1,) + (1,) * (len(dims) - 1 - dim))
    return loudness


def scatter_about(own_key, dims, width, most, cuts=(), held_as=jnp.bfloat16):
    result = width * jax.random.normal(own_key, dims, jnp.float32)
    if cuts:
        result = result * levels(own_key, dims, cuts, -0.22, 0.18)
    return jnp.clip(result, -most, most).astype(held_as)


def bell_draw_with(own_key, extent, width, most, cuts, heavy, held_as=jnp.bfloat16):
    result = width * jax.random.normal(own_key, extent, jnp.float32)
    if cuts:
        result = result * levels(own_key, extent, cuts, -0.22, 0.18)
    return jnp.clip(spiked(result, jax.random.fold_in(own_key, 3), *heavy), -most, most).astype(held_as)


def setup_inputs(seed: int = 0, part: int = 0) -> dict:
    splits = jax.random.split(jax.random.key(seed), 12)
    part_splits = jax.random.split(jax.random.fold_in(splits[11], part), 12)
    stored_hidden = bell_draw_with(part_splits[0], (N_SEQ, E_HALF, D), 1.0, 6.0, ((0, 2), (2, 8)), (2, 1, 8, 2.0))
    w_down_kv = scatter_about(splits[1], (D, C), D ** -0.5, 0.0625, ((0, 8),))
    kv_gain = jnp.clip(1.0 + 0.1 * jax.random.normal(splits[2], (KV_RANK,), jnp.float32), 0.5, 1.5).astype(jnp.bfloat16)
    evicted_blocks = draw_evicted_blocks(jax.random.fold_in(jax.random.fold_in(splits[11], part), 71), part)
    query_latent = scatter_about(part_splits[4], (Q, QL), 1.0, 6.0, ((0, 8),))
    w_up_q = scatter_about(splits[5], (QL, H * QK), QL ** -0.5, 0.15625, ((1, 8),))
    w_key_absorb = scatter_about(splits[6], (H, NOPE, KV_RANK), NOPE ** -0.5, 0.5, ((0, 8),))
    w_value = scatter_about(splits[7], (H, KV_RANK, VH), KV_RANK ** -0.5, 0.25, ((0, 8),))
    query_positions = touch_ends(jax.random.randint(part_splits[8], (Q,), S, 2 * S), jax.random.fold_in(part_splits[8], 1), S, (2 * S) - 1).astype(jnp.int32)
    prefix_lengths = draw_prefix_lengths(jax.random.fold_in(jax.random.fold_in(splits[11], part), 71), part)
    latent_cache = draw_latent_cache(jax.random.fold_in(jax.random.fold_in(splits[11], part), 71), part)
    return dict(stored_hidden=stored_hidden, w_down_kv=w_down_kv, kv_gain=kv_gain, evicted_blocks=evicted_blocks, query_latent=query_latent, w_up_q=w_up_q, w_key_absorb=w_key_absorb, w_value=w_value, query_positions=query_positions, prefix_lengths=prefix_lengths, latent_cache=latent_cache)


def rotate(values, positions):
    half_dim = values.shape[-1] // 2
    freqs = 10000.0 ** (jnp.arange(half_dim, dtype=jnp.float32) * (-2.0 / values.shape[-1]))
    angle = positions.astype(jnp.float32)[..., None] * freqs
    cosine = jnp.cos(angle)
    sine = jnp.sin(angle)
    first = values[..., :half_dim]
    second = values[..., half_dim:]
    return jnp.concatenate([first * cosine - second * sine, second * cosine + first * sine], axis=-1)

def reference(stored_hidden, w_down_kv, kv_gain, evicted_blocks, query_latent, w_up_q, w_key_absorb, w_value, query_positions, prefix_lengths, latent_cache):
    flat_hidden = stored_hidden.reshape(EVICTED, D)
    latent_raw = jnp.dot(flat_hidden, w_down_kv, preferred_element_type=jnp.float32)
    latent = latent_raw[:, :KV_RANK]
    mean_square = lax.optimization_barrier(jnp.mean(latent * latent, axis=-1, keepdims=True))
    normed = latent / jnp.sqrt(mean_square + 1e-06) * kv_gain.astype(jnp.float32)
    flat_index = jnp.arange(EVICTED, dtype=jnp.int32)
    key_position = (evicted_blocks[flat_index // BLK] * BLK + flat_index % BLK).astype(jnp.int32)
    rebuilt_flat = jnp.concatenate([normed, rotate(latent_raw[:, KV_RANK:], key_position)], axis=-1).astype(jnp.bfloat16)
    query_proj = jnp.dot(query_latent, w_up_q, preferred_element_type=jnp.float32).reshape(Q, H, QK)
    query_nope = query_proj[..., :NOPE].astype(jnp.bfloat16)
    absorbed = jnp.einsum('qhn,hnc->qhc', query_nope.astype(jnp.float32), w_key_absorb.astype(jnp.float32))
    rotated = rotate(query_proj[..., NOPE:], query_positions[:, None])
    query_full = (jnp.concatenate([absorbed, rotated], axis=-1) * QK ** (-0.5)).astype(jnp.bfloat16)
    cache_position = jnp.arange(S, dtype=jnp.int32)
    stale = jnp.any((cache_position // BLK)[:, None] == evicted_blocks[None, :], axis=1)
    keys_all = jnp.concatenate([latent_cache, rebuilt_flat], axis=0)
    keys_turned = keys_all.T
    values_all = keys_all[:, :KV_RANK]
    positions_all = jnp.concatenate([cache_position, key_position], axis=0)
    valid_all = jnp.concatenate([jnp.logical_not(stale), jnp.ones((EVICTED,), dtype=jnp.bool_)], axis=0)
    request_of = jnp.arange(Q, dtype=jnp.int32) // (Q // REQUESTS)
    limit = prefix_lengths[request_of]
    allowed = valid_all[None, :] & (positions_all[None, :] < limit[:, None])

    def one_head(pair):
        query_head, value_head = pair
        scores = jnp.dot(query_head, keys_turned, preferred_element_type=jnp.float32)
        largest = lax.optimization_barrier(jnp.max(jnp.where(allowed, scores, -1e+30), axis=-1, keepdims=True))
        prob = jnp.where(allowed, jnp.exp(scores - largest), 0.0)
        denom = lax.optimization_barrier(jnp.sum(prob, axis=-1, keepdims=True))
        latent_out = jnp.dot(prob.astype(jnp.bfloat16), values_all, preferred_element_type=jnp.float32) / denom
        return jnp.dot(latent_out, value_head.astype(jnp.float32), precision=lax.Precision.HIGHEST).astype(jnp.bfloat16)
    outputs = lax.map(one_head, (jnp.transpose(query_full, (1, 0, 2)), w_value))
    attended = jnp.transpose(outputs, (1, 0, 2)).reshape(Q, H * VH)
    rebuilt = rebuilt_flat.reshape(N_SEQ, E_HALF, C)
    return (rebuilt, attended)
```

```python
import functools
import numpy as np
import jax
import jax.numpy as jnp
from jax import lax
from jax.experimental import pallas as pl
from jax.experimental.pallas import tpu as pltpu
from jax.sharding import PartitionSpec as P

BLK = 128
NEG = -1e30
FLOOR = -1e20
FAR = 2**30
NORM_EPS = 1e-06
F32 = jnp.float32
BF16 = jnp.bfloat16
MESH = pl.DeviceIdType.MESH


def swap_halves(x):
    half = x.shape[-1] // 2
    return jnp.concatenate([x[:, half:], x[:, :half]], axis=-1)


def trig(pos, freq, rope_dim):
    angle = pos.astype(F32) * freq
    lane = lax.broadcasted_iota(jnp.int32, angle.shape, 1)
    sine = jnp.sin(angle)
    return jnp.cos(angle), jnp.where(lane < rope_dim // 2, -sine, sine)


def kernel(
    cfg,
    eb_hbm, qp_hbm, pf_hbm, freq_hbm, gain_hbm,
    hid_hbm, wd_hbm, ql_hbm, wq_hbm, wk_hbm, wv_hbm, kc_hbm,
    reb_ref, att_ref,
    eb_ref, qp_ref, pf_ref, freq_ref, gain_ref,
    hid, wd, ql, qlf, wq, wk, wv, kc,
    qf, part, rsum, rown, rall, fx, sb, mx_s, l_s, acc_s, osend, orecv,
    i_sem, w_sem, q_sem, c_sem, ql_ss, ql_rs, rs_ss, rs_rs, ag_ss, ag_rs, ex_ss, ex_rs,
):
    T, heads, nope, rank, rope_dim, Q, requests, nq, nb, bk, ng, kt = cfg
    me = lax.axis_index("tensor")
    sq = lax.axis_index("seq")
    other = 1 - sq
    head_qk = nope + rope_dim
    piece = ql_hbm.shape[0]
    half_rows = hid.shape[0]
    local = half_rows // T
    R = heads * Q
    n_evicted = eb_ref.shape[0]
    hq = heads // nq
    width = rank + rope_dim
    kd, nk = kc.shape
    extra = kd - width

    def far(d):
        return lax.rem(me + d, T)

    def near(d):
        return lax.rem(me + T - d, T)

    barrier = pltpu.get_barrier_semaphore()
    for d in range(1, T):
        pl.semaphore_signal(barrier, inc=1, device_id={"tensor": far(d)}, device_id_type=MESH)
    pl.semaphore_signal(barrier, inc=1, device_id={"seq": other}, device_id_type=MESH)

    small = [
        pltpu.make_async_copy(src, dst, i_sem.at[n])
        for n, (src, dst) in enumerate((
            (eb_hbm, eb_ref), (qp_hbm, qp_ref), (pf_hbm, pf_ref),
            (freq_hbm, freq_ref), (gain_hbm, gain_ref),
        ))
    ]
    own_q = pltpu.make_async_copy(ql_hbm, ql.at[me], w_sem.at[0])
    c_hid = pltpu.make_async_copy(hid_hbm.at[0], hid, w_sem.at[1])
    c_wd = pltpu.make_async_copy(wd_hbm, wd, w_sem.at[2])
    c_wk = pltpu.make_async_copy(wk_hbm, wk, w_sem.at[3])
    c_wv = pltpu.make_async_copy(wv_hbm, wv, w_sem.at[4])
    wide = hq * head_qk
    c_wq = [
        pltpu.make_async_copy(
            wq_hbm.at[:, pl.ds(i * wide, wide)], wq.at[:, pl.ds(i * wide, wide)], q_sem.at[i]
        )
        for i in range(nq)
    ]
    c_kc = [
        pltpu.make_async_copy(
            kc_hbm.at[:, pl.ds(i * bk, bk)], kc.at[pl.ds(0, width), pl.ds(i * bk, bk)],
            c_sem.at[i],
        )
        for i in range(nb)
    ]

    own_q.start()
    for c in small:
        c.start()
    c_hid.start()
    c_wd.start()
    for c in c_wq:
        c.start()
    c_wk.start()
    for c in c_kc:
        c.start()
    c_wv.start()

    def ql_copy(d, slot):
        return pltpu.make_async_remote_copy(
            src_ref=ql_hbm, dst_ref=ql.at[slot], send_sem=ql_ss.at[d], recv_sem=ql_rs.at[d],
            device_id={"tensor": far(d)}, device_id_type=MESH,
        )

    def rs_copy(d, slot):
        return pltpu.make_async_remote_copy(
            src_ref=part.at[far(d)], dst_ref=rsum.at[slot], send_sem=rs_ss.at[d],
            recv_sem=rs_rs.at[d], device_id={"tensor": far(d)}, device_id_type=MESH,
        )

    def ag_copy(d, slot):
        return pltpu.make_async_remote_copy(
            src_ref=rown, dst_ref=rall.at[slot], send_sem=ag_ss.at[d], recv_sem=ag_rs.at[d],
            device_id={"tensor": far(d)}, device_id_type=MESH,
        )

    pl.semaphore_wait(barrier, T)
    for d in range(1, T):
        ql_copy(d, me).start()

    for c in small:
        c.wait()
    freq = freq_ref[...]
    qrow = lax.broadcasted_iota(jnp.int32, (Q, 1), 0)
    qpos = lax.fori_loop(
        0, Q, lambda i, v: jnp.where(qrow == i, qp_ref[i], v), jnp.zeros((Q, 1), jnp.int32)
    )
    qcos, qsin = trig(qpos, freq, rope_dim)
    per = Q // requests
    belongs = lax.broadcasted_iota(jnp.int32, (Q, extra), 0) // per
    chosen = jnp.where(
        belongs == lax.broadcasted_iota(jnp.int32, (Q, extra), 1), 1.0, 0.0
    )
    flat0 = sq * half_rows + me * local
    rpos = (
        eb_ref[flat0 // BLK] * BLK + flat0 % BLK
        + lax.broadcasted_iota(jnp.int32, (local, 1), 0)
    )
    rcos, rsin = trig(rpos, freq, rope_dim)

    def limits(axis, shape):
        index = lax.broadcasted_iota(jnp.int32, shape, axis)
        limit = jnp.full(shape, FAR, jnp.int32)
        for r in range(requests):
            limit = jnp.where(index == r, pf_ref[r], limit)
        return jnp.where(index < requests, limit, 2 * (FAR - 1) + 1)

    pos = sq * nk + lax.broadcasted_iota(jnp.int32, (1, nk), 1)
    eff = pos
    for e in range(n_evicted):
        first = eb_ref[e] * BLK
        eff = jnp.where((pos >= first) & (pos < first + BLK), FAR, eff)
    kc[width:, :] = jnp.where(eff < limits(0, (extra, 1)), 0.0, NEG).astype(BF16)

    flat = sq * half_rows + lax.broadcasted_iota(jnp.int32, (half_rows, 1), 0)
    fpos = flat
    for e in range(n_evicted):
        inside = (flat >= e * BLK) & (flat < (e + 1) * BLK)
        fpos = jnp.where(inside, eb_ref[e] * BLK + flat - e * BLK, fpos)
    fbias = jnp.where(fpos < limits(1, (1, extra)), 0.0, NEG)

    c_hid.wait()
    c_wd.wait()
    partial = lax.dot_general(
        hid[...], wd[...], (((1,), (1,)), ((), ())), preferred_element_type=F32
    )
    for t in range(T):
        part[t] = partial[t * local:(t + 1) * local, :]
    rsum[me] = part[me]

    own_q.wait()
    for c in c_wq:
        c.wait()
    c_wk.wait()
    for d in range(1, T):
        ql_copy(d, near(d)).wait_recv()
    for d in range(1, T):
        rs_copy(d, me).start()
    for t in range(T):
        qlf[t * piece:(t + 1) * piece, :] = ql[t].astype(F32)
    queries = qlf[...].astype(BF16)
    scale = float(head_qk) ** (-0.5)

    def project(i):
        return jnp.dot(
            queries, wq[:, i * wide:(i + 1) * wide], preferred_element_type=F32
        )

    def absorb(i, proj):
        for j in range(hq):
            h = i * hq + j
            q_nope = proj[:, j * head_qk:j * head_qk + nope].astype(BF16)
            q_rope = proj[:, j * head_qk + nope:(j + 1) * head_qk]
            absorbed = jnp.dot(q_nope, wk[h], preferred_element_type=F32)
            qf[h * Q:(h + 1) * Q, :rank] = (absorbed * scale).astype(BF16)
            turned = q_rope * qcos + swap_halves(q_rope) * qsin
            qf[h * Q:(h + 1) * Q, rank:] = jnp.concatenate(
                [turned * scale, chosen], axis=-1
            ).astype(BF16)

    ahead = project(0)
    for i in range(1, nq):
        later = project(i)
        absorb(i - 1, ahead)
        ahead = later
    absorb(nq - 1, ahead)

    for c in c_kc:
        c.wait()
    nt = nk // kt
    LANES = 128
    early = max(1, (5 * nt) // 8)

    def fold(op, x):
        parts = [x[:, c * LANES:(c + 1) * LANES] for c in range(x.shape[1] // LANES)]
        while len(parts) > 1:
            parts = [
                op(parts[n], parts[n + 1]) if n + 1 < len(parts) else parts[n]
                for n in range(0, len(parts), 2)
            ]
        return parts[0]

    def score(t):
        cols = slice(t * kt, (t + 1) * kt)
        s = jnp.dot(qf[...], kc[:, cols], preferred_element_type=F32)
        sb[:, cols] = s
        top = fold(jnp.maximum, s)
        mx_s[...] = top if t == 0 else jnp.maximum(mx_s[...], top)

    for t in range(early):
        score(t)

    for d in range(1, T):
        rs_copy(d, near(d)).wait_recv()
    summed = rsum[0]
    for t in range(1, T):
        summed = summed + rsum[t]
    latent = summed[:, :rank]
    mean_square = jnp.mean(latent * latent, axis=-1, keepdims=True)
    normed = latent / jnp.sqrt(mean_square + NORM_EPS) * gain_ref[...].astype(F32).reshape(1, rank)
    tail = summed[:, rank:]
    turned = tail * rcos + swap_halves(tail) * rsin
    rown[:, :rank] = normed.astype(BF16)
    rown[:, rank:] = turned.astype(BF16)
    reb_ref[0] = rown[...]
    rall[me] = rown[...]
    for d in range(1, T):
        ag_copy(d, me).start()

    for t in range(early, nt):
        score(t)

    m_a = jnp.maximum(jnp.max(mx_s[...], axis=1, keepdims=True), FLOOR)
    mx_s[...] = jnp.broadcast_to(m_a, mx_s.shape)

    def weigh(t):
        top = mx_s[...]
        ps = [
            jnp.exp(sb[:, c:c + LANES] - top) for c in range(t * kt, (t + 1) * kt, LANES)
        ]
        p = jnp.concatenate(ps, axis=-1)
        total = fold(jnp.add, p)
        l_s[...] = total if t == 0 else l_s[...] + total
        out = lax.dot_general(
            p.astype(BF16), kc[:rank, t * kt:(t + 1) * kt], (((1,), (1,)), ((), ())),
            preferred_element_type=F32,
        )
        acc_s[...] = out if t == 0 else acc_s[...] + out

    for t in range(nt):
        weigh(t)

    for d in range(1, T):
        ag_copy(d, near(d)).wait_recv()
    fresh = jnp.concatenate([rall[t].astype(F32) for t in range(T)], axis=0)
    fx[:, :rank] = fresh[:, :rank].astype(BF16)
    fx[:, rank:] = jnp.concatenate([fresh[:, rank:], fbias], axis=-1).astype(BF16)
    s_f = lax.dot_general(
        qf[...], fx[...], (((1,), (1,)), ((), ())), preferred_element_type=F32
    )
    m_f = jnp.maximum(jnp.max(s_f, axis=1, keepdims=True), FLOOR)
    p_f = jnp.exp(s_f - m_f)
    l_f = jnp.sum(p_f, axis=1, keepdims=True)
    acc_f = jnp.dot(p_f.astype(BF16), fx[:, :rank], preferred_element_type=F32)
    l_a = jnp.sum(l_s[...], axis=1, keepdims=True)
    m_own = jnp.maximum(m_a, m_f)
    w_a, w_f = jnp.exp(m_a - m_own), jnp.exp(m_f - m_own)
    l_own = l_a * w_a + l_f * w_f

    vh = wv.shape[2]
    gcols = (heads // ng) * vh

    def ex_copy(g):
        cols = pl.ds(g * gcols, gcols) if g < ng else pl.ds(heads * vh, 128)
        return pltpu.make_async_remote_copy(
            src_ref=osend.at[:, cols], dst_ref=orecv.at[:, cols], send_sem=ex_ss.at[g],
            recv_sem=ex_rs.at[g], device_id={"seq": other}, device_id_type=MESH,
        )

    lane = lax.broadcasted_iota(jnp.int32, (Q, 128), 1)
    stats = jnp.zeros((Q, 128), F32)
    for h in range(heads):
        stats = jnp.where(lane == h, m_own[h * Q:(h + 1) * Q, :], stats)
        stats = jnp.where(lane == heads + h, l_own[h * Q:(h + 1) * Q, :], stats)
    osend[:, heads * vh:] = stats
    ex_copy(ng).start()
    c_wv.wait()
    for g in range(ng):
        for h in range(g * (heads // ng), (g + 1) * (heads // ng)):
            rows = slice(h * Q, (h + 1) * Q)
            a = acc_s[rows, :] * w_a[rows, :] + acc_f[rows, :] * w_f[rows, :]
            high = a.astype(BF16)
            low = (a - high.astype(F32)).astype(BF16)
            both = jnp.dot(
                jnp.concatenate([high, low], axis=0), wv[h], preferred_element_type=F32
            )
            osend[:, h * vh:(h + 1) * vh] = both[:Q] + both[Q:]
        ex_copy(g).start()

    ex_copy(ng).wait_recv()
    theirs = orecv[:, heads * vh:]
    m_a, m_b = stats[:, :heads], theirs[:, :heads]
    joint = jnp.maximum(m_a, m_b)
    e_a, e_b = jnp.exp(m_a - joint), jnp.exp(m_b - joint)
    total = e_a * stats[:, heads:2 * heads] + e_b * theirs[:, heads:2 * heads]
    e_a, e_b = e_a / total, e_b / total
    for g in range(ng):
        ex_copy(g).wait_recv()
        for h in range(g * (heads // ng), (g + 1) * (heads // ng)):
            cols = slice(h * vh, (h + 1) * vh)
            att_ref[:, cols] = (
                e_a[:, h:h + 1] * osend[:, cols] + e_b[:, h:h + 1] * orecv[:, cols]
            ).astype(BF16)

    for d in range(1, T):
        ql_copy(d, me).wait_send()
        rs_copy(d, me).wait_send()
        ag_copy(d, me).wait_send()
    for g in range(ng + 1):
        ex_copy(g).wait_send()


def hand_over(reb_in, att_in, reb_out, att_out):
    reb_out[...] = reb_in[...]
    att_out[...] = att_in[...]


def body(
    stored_hidden, w_down_kv, kv_gain, evicted_blocks, query_latent, w_up_q,
    w_key_absorb, w_value, query_positions, prefix_lengths, latent_cache,
):
    T = lax.axis_size("tensor")
    rank = kv_gain.shape[0]
    heads, nope = w_key_absorb.shape[:2]
    width = w_down_kv.shape[1]
    rope_dim = width - rank
    Q = query_positions.shape[0]
    requests = prefix_lengths.shape[0]
    half_rows = stored_hidden.shape[1]
    local = half_rows // T
    cache_rows = latent_cache.shape[0]
    bk = min(2048, cache_rows)
    nb = cache_rows // bk
    kt = min(1024, cache_rows)
    kd = rank + -(-(rope_dim + requests) // 128) * 128
    nq = max(1, heads // 4)
    ng = max(1, heads // 4)
    vh = w_value.shape[2]
    R = heads * Q
    half = np.arange(rope_dim // 2, dtype=np.float64) * (-2.0 / rope_dim)
    freq = jnp.asarray(np.tile(10000.0 ** half, 2)[None, :].astype(np.float32))
    cfg = (T, heads, nope, rank, rope_dim, Q, requests, nq, nb, bk, ng, kt)
    vmem = pl.BlockSpec(memory_space=pltpu.VMEM)
    hbm = pl.BlockSpec(memory_space=pl.ANY)
    dma = pltpu.SemaphoreType.DMA
    outs = pl.pallas_call(
        functools.partial(kernel, cfg),
        name="rebuild_attend",
        out_shape=(
            jax.ShapeDtypeStruct((1, local, width), BF16),
            jax.ShapeDtypeStruct((Q, heads * vh), BF16),
        ),
        in_specs=[hbm] * 12,
        out_specs=(vmem, vmem),
        scratch_shapes=[
            pltpu.SMEM(evicted_blocks.shape, jnp.int32),
            pltpu.SMEM(query_positions.shape, jnp.int32),
            pltpu.SMEM(prefix_lengths.shape, jnp.int32),
            pltpu.VMEM(freq.shape, F32),
            pltpu.VMEM(kv_gain.shape, BF16),
            pltpu.VMEM((half_rows, w_down_kv.shape[0]), BF16),
            pltpu.VMEM(w_down_kv.shape[::-1], BF16),
            pltpu.VMEM((T,) + query_latent.shape, BF16),
            pltpu.VMEM((Q, query_latent.shape[1]), F32),
            pltpu.VMEM(w_up_q.shape, BF16),
            pltpu.VMEM(w_key_absorb.shape, BF16),
            pltpu.VMEM(w_value.shape, BF16),
            pltpu.VMEM((kd, cache_rows), BF16),
            pltpu.VMEM((R, kd), BF16),
            pltpu.VMEM((T, local, width), F32),
            pltpu.VMEM((T, local, width), F32),
            pltpu.VMEM((local, width), BF16),
            pltpu.VMEM((T, local, width), BF16),
            pltpu.VMEM((half_rows, kd), BF16),
            pltpu.VMEM((R, cache_rows), F32),
            pltpu.VMEM((R, 128), F32),
            pltpu.VMEM((R, 128), F32),
            pltpu.VMEM((R, rank), F32),
            pltpu.VMEM((Q, heads * vh + 128), F32),
            pltpu.VMEM((Q, heads * vh + 128), F32),
            dma((5,)), dma((5,)), dma((nq,)), dma((nb,)),
            dma((T,)), dma((T,)), dma((T,)), dma((T,)), dma((T,)), dma((T,)),
            dma((ng + 1,)), dma((ng + 1,)),
        ],
        compiler_params=pltpu.CompilerParams(
            collective_id=0, has_side_effects=True, vmem_limit_bytes=60 * 1024 * 1024
        ),
    )(
        evicted_blocks, query_positions, prefix_lengths, freq, kv_gain,
        stored_hidden, w_down_kv.T, query_latent, w_up_q, w_key_absorb, w_value, latent_cache.T,
    )
    return pl.pallas_call(
        hand_over,
        name="hand_over",
        out_shape=tuple(jax.ShapeDtypeStruct(o.shape, o.dtype) for o in outs),
        in_specs=[vmem] * 2,
        out_specs=(vmem, vmem),
    )(*outs)


def solution(mesh):
    placed = (
        P(("groups", "seq"), None, "tensor"),
        P("tensor", None),
        P(),
        P("groups"),
        P(("groups", "tensor"), None),
        P(None, "tensor"),
        P("tensor", None, None),
        P("tensor", None, None),
        P("groups"),
        P("groups"),
        P(("groups", "seq"), None),
    )
    return jax.shard_map(
        body,
        mesh=mesh,
        in_specs=placed,
        out_specs=(P(("groups", "seq"), "tensor", None), P("groups", "tensor")),
        check_vma=False,
    )
```

```python
import functools
import numpy as np
import jax
import jax.numpy as jnp
from jax import lax
from jax.experimental import pallas as pl
from jax.experimental.pallas import tpu as pltpu
from jax.sharding import PartitionSpec as P

BLK = 128
NEG = -1e30
FLOOR = -1e20
FAR = 2**30
NORM_EPS = 1e-06
F32 = jnp.float32
BF16 = jnp.bfloat16
MESH = pl.DeviceIdType.MESH


def swap_halves(x):
    half = x.shape[-1] // 2
    return jnp.concatenate([x[:, half:], x[:, :half]], axis=-1)


def trig(pos, freq, rope_dim):
    angle = pos.astype(F32) * freq
    lane = lax.broadcasted_iota(jnp.int32, angle.shape, 1)
    sine = jnp.sin(angle)
    return jnp.cos(angle), jnp.where(lane < rope_dim // 2, -sine, sine)


def kernel(
    cfg,
    eb_hbm, qp_hbm, pf_hbm, freq_hbm, gain_hbm,
    hid_hbm, wd_hbm, ql_hbm, wq_hbm, wk_hbm, wv_hbm, kc_hbm,
    reb_ref, att_ref,
    eb_ref, qp_ref, pf_ref, freq_ref, gain_ref,
    hid, wd, ql, qlf, wq, wk, wv, kc,
    qf, part, rsum, rown, rall, fx, sb, pb, mx_s, l_s, acc_s, osend, orecv,
    i_sem, w_sem, q_sem, c_sem, ql_ss, ql_rs, rs_ss, rs_rs, ag_ss, ag_rs,
    ex_ss, ex_rs, qx_ss, qx_rs,
):
    T, nope, rank, rope_dim, Q, requests, split, nq, nb, bk, ng, kt, ke = cfg
    me = lax.axis_index("tensor")
    sq = lax.axis_index("seq")
    other = 1 - sq
    head_qk = nope + rope_dim
    piece = ql_hbm.shape[0]
    half_rows = hid.shape[0]
    local = half_rows // T
    n_evicted = eb_ref.shape[0]
    hh, vh = wv.shape[1], wv.shape[3]
    hq = wk.shape[0] // nq
    width = rank + rope_dim
    kd, nk = kc.shape
    extra = kd - width
    halves = (sq, other) if split else (0, 1)
    facing = (1, 0) if split else (0, 1)

    def far(d):
        return lax.rem(me + d, T)

    def near(d):
        return lax.rem(me + T - d, T)

    barrier = pltpu.get_barrier_semaphore()
    for d in range(1, T):
        pl.semaphore_signal(barrier, inc=1, device_id={"tensor": far(d)}, device_id_type=MESH)
    pl.semaphore_signal(barrier, inc=1, device_id={"seq": other}, device_id_type=MESH)

    small = [
        pltpu.make_async_copy(src, dst, i_sem.at[n])
        for n, (src, dst) in enumerate((
            (eb_hbm, eb_ref), (qp_hbm, qp_ref), (pf_hbm, pf_ref),
            (freq_hbm, freq_ref), (gain_hbm, gain_ref),
        ))
    ]
    own_q = pltpu.make_async_copy(ql_hbm, ql.at[me], w_sem.at[0])
    c_hid = pltpu.make_async_copy(hid_hbm.at[0], hid, w_sem.at[1])
    c_wd = pltpu.make_async_copy(wd_hbm, wd, w_sem.at[2])
    wide = hq * head_qk
    first_head = sq * hh if split else 0
    c_wk = pltpu.make_async_copy(wk_hbm.at[pl.ds(first_head, nq * hq)], wk, w_sem.at[3])
    c_wv = [
        pltpu.make_async_copy(wv_hbm.at[pl.ds(halves[s] * hh, hh)], wv.at[s], w_sem.at[4 + s])
        for s in range(2)
    ]

    def c_wq_of(i):
        start = sq * (nq * wide) + i * wide if split else i * wide
        if split:
            start = pl.multiple_of(start, 128)
        return pltpu.make_async_copy(
            wq_hbm.at[:, pl.ds(start, wide)], wq.at[:, pl.ds(i * wide, wide)], q_sem.at[i]
        )

    c_wq = [c_wq_of(i) for i in range(nq)]
    c_kc = [
        pltpu.make_async_copy(
            kc_hbm.at[:, pl.ds(i * bk, bk)], kc.at[pl.ds(0, width), pl.ds(i * bk, bk)],
            c_sem.at[i],
        )
        for i in range(nb)
    ]

    own_q.start()
    for c in small:
        c.start()
    c_hid.start()
    c_wd.start()
    for c in c_wq:
        c.start()
    c_wk.start()
    for c in c_kc:
        c.start()
    for c in c_wv:
        c.start()

    def ql_copy(d, slot):
        return pltpu.make_async_remote_copy(
            src_ref=ql_hbm, dst_ref=ql.at[slot], send_sem=ql_ss.at[d], recv_sem=ql_rs.at[d],
            device_id={"tensor": far(d)}, device_id_type=MESH,
        )

    def rs_copy(d, slot):
        return pltpu.make_async_remote_copy(
            src_ref=part.at[far(d)], dst_ref=rsum.at[slot], send_sem=rs_ss.at[d],
            recv_sem=rs_rs.at[d], device_id={"tensor": far(d)}, device_id_type=MESH,
        )

    def qx_copy(i):
        size = hq * Q
        return pltpu.make_async_remote_copy(
            src_ref=qf.at[pl.ds(i * size, size)],
            dst_ref=qf.at[pl.ds((nq + i) * size, size)], send_sem=qx_ss.at[i],
            recv_sem=qx_rs.at[i], device_id={"seq": other}, device_id_type=MESH,
        )

    def ag_copy(d, slot):
        return pltpu.make_async_remote_copy(
            src_ref=rown, dst_ref=rall.at[slot], send_sem=ag_ss.at[d], recv_sem=ag_rs.at[d],
            device_id={"tensor": far(d)}, device_id_type=MESH,
        )

    pl.semaphore_wait(barrier, T)
    for d in range(1, T):
        ql_copy(d, me).start()

    for c in small:
        c.wait()
    freq = freq_ref[...]
    qrow = lax.broadcasted_iota(jnp.int32, (Q, 1), 0)
    qpos = lax.fori_loop(
        0, Q, lambda i, v: jnp.where(qrow == i, qp_ref[i], v), jnp.zeros((Q, 1), jnp.int32)
    )
    qcos, qsin = trig(qpos, freq, rope_dim)
    per = Q // requests
    belongs = lax.broadcasted_iota(jnp.int32, (Q, extra), 0) // per
    chosen = jnp.where(
        belongs == lax.broadcasted_iota(jnp.int32, (Q, extra), 1), 1.0, 0.0
    )
    flat0 = sq * half_rows + me * local
    rpos = (
        eb_ref[flat0 // BLK] * BLK + flat0 % BLK
        + lax.broadcasted_iota(jnp.int32, (local, 1), 0)
    )
    rcos, rsin = trig(rpos, freq, rope_dim)

    def limits(axis, shape):
        index = lax.broadcasted_iota(jnp.int32, shape, axis)
        limit = jnp.full(shape, FAR, jnp.int32)
        for r in range(requests):
            limit = jnp.where(index == r, pf_ref[r], limit)
        return jnp.where(index < requests, limit, 2 * (FAR - 1) + 1)

    pos = sq * nk + lax.broadcasted_iota(jnp.int32, (1, nk), 1)
    eff = pos
    for e in range(n_evicted):
        first = eb_ref[e] * BLK
        eff = jnp.where((pos >= first) & (pos < first + BLK), FAR, eff)
    kc[width:, :] = jnp.where(eff < limits(0, (extra, 1)), 0.0, NEG).astype(BF16)

    flat = sq * half_rows + lax.broadcasted_iota(jnp.int32, (half_rows, 1), 0)
    fpos = flat
    for e in range(n_evicted):
        inside = (flat >= e * BLK) & (flat < (e + 1) * BLK)
        fpos = jnp.where(inside, eb_ref[e] * BLK + flat - e * BLK, fpos)
    fbias = jnp.where(fpos < limits(1, (1, extra)), 0.0, NEG)

    c_hid.wait()
    c_wd.wait()
    partial = lax.dot_general(
        hid[...], wd[...], (((1,), (1,)), ((), ())), preferred_element_type=F32
    )
    for t in range(T):
        part[t] = partial[t * local:(t + 1) * local, :]
    rsum[me] = part[me]
    for d in range(1, T):
        rs_copy(d, me).start()

    own_q.wait()
    for c in c_wq:
        c.wait()
    c_wk.wait()
    for d in range(1, T):
        ql_copy(d, near(d)).wait_recv()
    for t in range(T):
        qlf[t * piece:(t + 1) * piece, :] = ql[t].astype(F32)
    queries = qlf[...].astype(BF16)
    scale = float(head_qk) ** (-0.5)

    def project(i):
        return jnp.dot(
            queries, wq[:, i * wide:(i + 1) * wide], preferred_element_type=F32
        )

    def absorb(i, proj):
        for j in range(hq):
            slot, h = divmod(i * hq + j, hh)
            at = slot * hh * Q + h * Q
            rows = slice(at, at + Q)
            q_nope = proj[:, j * head_qk:j * head_qk + nope].astype(BF16)
            q_rope = proj[:, j * head_qk + nope:(j + 1) * head_qk]
            absorbed = jnp.dot(q_nope, wk[i * hq + j], preferred_element_type=F32)
            qf[rows, :rank] = (absorbed * scale).astype(BF16)
            turned = q_rope * qcos + swap_halves(q_rope) * qsin
            qf[rows, rank:] = jnp.concatenate(
                [turned * scale, chosen], axis=-1
            ).astype(BF16)

    ahead = project(0)
    for i in range(1, nq):
        later = project(i)
        absorb(i - 1, ahead)
        ahead = later
        if split:
            qx_copy(i - 1).start()
    absorb(nq - 1, ahead)
    if split:
        qx_copy(nq - 1).start()

    for c in c_kc:
        c.wait()
    nt, ne = nk // kt, nk // ke
    kept = pb.shape[1] // ke
    LANES = 128

    def fold(op, x):
        parts = [x[:, c * LANES:(c + 1) * LANES] for c in range(x.shape[1] // LANES)]
        while len(parts) > 1:
            parts = [
                op(parts[n], parts[n + 1]) if n + 1 < len(parts) else parts[n]
                for n in range(0, len(parts), 2)
            ]
        return parts[0]

    R = hh * Q
    own, theirs, both = slice(0, R), slice(R, 2 * R), slice(0, 2 * R)

    def score(rows, t):
        cols = slice(t * kt, (t + 1) * kt)
        dots = jnp.dot(qf[rows, :], kc[:, cols], preferred_element_type=F32)
        sb[rows, cols] = dots
        top = fold(jnp.maximum, dots)
        mx_s[rows, :] = top if t == 0 else jnp.maximum(mx_s[rows, :], top)

    def highest(rows):
        top = jnp.maximum(jnp.max(mx_s[rows, :], axis=1, keepdims=True), FLOOR)
        mx_s[rows, :] = jnp.broadcast_to(top, mx_s[rows, :].shape)
        return top

    def weigh(rows, t):
        cols = slice(t * ke, (t + 1) * ke)
        top = mx_s[rows, :]
        ps = [jnp.exp(sb[rows, c:c + LANES] - top) for c in range(t * ke, (t + 1) * ke, LANES)]
        p = jnp.concatenate(ps, axis=-1)
        total = fold(jnp.add, p)
        l_s[rows, :] = total if t == 0 else l_s[rows, :] + total
        out = lax.dot_general(
            p.astype(BF16), kc[:rank, cols], (((1,), (1,)), ((), ())),
            preferred_element_type=F32,
        )
        acc_s[rows, :] = out if t == 0 else acc_s[rows, :] + out

    def ahead_of(rows, t):
        cols = slice(t * ke, (t + 1) * ke)
        top = mx_s[rows, :]
        ps = [jnp.exp(sb[rows, c:c + LANES] - top) for c in range(t * ke, (t + 1) * ke, LANES)]
        p = jnp.concatenate(ps, axis=-1)
        l_s[rows, :] = l_s[rows, :] + fold(jnp.add, p)
        n = t - (ne - kept)
        pb[rows, n * ke:(n + 1) * ke] = p.astype(BF16)

    def finish(rows):
        out = lax.dot_general(
            pb[rows, :], kc[:rank, (ne - kept) * ke:], (((1,), (1,)), ((), ())),
            preferred_element_type=F32,
        )
        acc_s[rows, :] = acc_s[rows, :] + out

    soon = max(1, (8 * nt) // 8)
    for t in range(soon):
        score(own, t)

    for d in range(1, T):
        rs_copy(d, near(d)).wait_recv()
    summed = rsum[0]
    for t in range(1, T):
        summed = summed + rsum[t]
    latent = summed[:, :rank]
    mean_square = jnp.mean(latent * latent, axis=-1, keepdims=True)
    normed = latent / jnp.sqrt(mean_square + NORM_EPS) * gain_ref[...].astype(F32).reshape(1, rank)
    tail = summed[:, rank:]
    turned = tail * rcos + swap_halves(tail) * rsin
    rown[:, :rank] = normed.astype(BF16)
    rown[:, rank:] = turned.astype(BF16)
    rall[me] = rown[...]
    for d in range(1, T):
        ag_copy(d, me).start()
    reb_ref[0] = rown[...]

    if split:
        for i in range(nq):
            qx_copy(i).wait_recv()
    for t in range(soon, nt):
        score(own, t)
    for t in range(nt):
        score(theirs, t)
    m_a = jnp.concatenate([highest(own), highest(theirs)], axis=0)
    for t in range(ne - kept):
        weigh(both, t)
    for t in range(ne - kept, ne):
        ahead_of(both, t)

    for d in range(1, T):
        ag_copy(d, near(d)).wait_recv()
    for c in c_wv:
        c.wait()
    fresh = jnp.concatenate([rall[t].astype(F32) for t in range(T)], axis=0)
    fx[:, :rank] = fresh[:, :rank].astype(BF16)
    fx[:, rank:] = jnp.concatenate([fresh[:, rank:], fbias], axis=-1).astype(BF16)

    s_f = lax.dot_general(
        qf[...], fx[...], (((1,), (1,)), ((), ())), preferred_element_type=F32
    )
    m_f = jnp.maximum(jnp.max(s_f, axis=1, keepdims=True), FLOOR)
    p_f = jnp.exp(s_f - m_f)
    l_f = jnp.sum(p_f, axis=1, keepdims=True)
    acc_f = jnp.dot(p_f.astype(BF16), fx[:, :rank], preferred_element_type=F32)
    m_own = jnp.maximum(m_a, m_f)
    w_a, w_f = jnp.exp(m_a - m_own), jnp.exp(m_f - m_own)

    def share(s):
        rows = slice(s * R, (s + 1) * R)
        l_own = jnp.sum(l_s[rows, :], axis=1, keepdims=True) * w_a[rows, :]
        l_own = l_own + l_f[rows, :] * w_f[rows, :]
        lane = lax.broadcasted_iota(jnp.int32, (Q, 128), 1)
        stats = jnp.zeros((Q, 128), F32)
        for h in range(hh):
            at = s * R + h * Q
            stats = jnp.where(lane == h, m_own[at:at + Q, :], stats)
            stats = jnp.where(lane == hh + h, l_own[h * Q:(h + 1) * Q, :], stats)
        osend[s, :, hh * vh:] = stats

    def expand(s, g):
        for h in range(g * (hh // ng), (g + 1) * (hh // ng)):
            rows = slice(s * R + h * Q, s * R + (h + 1) * Q)
            a = acc_s[rows, :] * w_a[rows, :] + acc_f[rows, :] * w_f[rows, :]
            high = a.astype(BF16)
            low = (a - high.astype(F32)).astype(BF16)
            both = jnp.dot(
                jnp.concatenate([high, low], axis=0), wv[s, h], preferred_element_type=F32
            )
            osend[s, :, h * vh:(h + 1) * vh] = both[:Q] + both[Q:]

    gcols = (hh // ng) * vh

    def cols_of(g):
        return pl.ds(g * gcols, gcols) if g < ng else pl.ds(hh * vh, 128)

    def ex_copy(s, g):
        n = s * (ng + 1) + g
        return pltpu.make_async_remote_copy(
            src_ref=osend.at[s, :, cols_of(g)], dst_ref=orecv.at[facing[s], :, cols_of(g)],
            send_sem=ex_ss.at[n], recv_sem=ex_rs.at[facing[s] * (ng + 1) + g],
            device_id={"seq": other}, device_id_type=MESH,
        )

    s_f = lax.dot_general(
        qf[...], fx[...], (((1,), (1,)), ((), ())), preferred_element_type=F32
    )
    m_f = jnp.maximum(jnp.max(s_f, axis=1, keepdims=True), FLOOR)
    p_f = jnp.exp(s_f - m_f)
    l_f = jnp.sum(p_f, axis=1, keepdims=True)
    acc_f = jnp.dot(p_f.astype(BF16), fx[:, :rank], preferred_element_type=F32)
    m_own = jnp.maximum(m_a, m_f)
    w_a, w_f = jnp.exp(m_a - m_own), jnp.exp(m_f - m_own)

    def share(s):
        rows = slice(s * R, (s + 1) * R)
        l_own = jnp.sum(l_s[rows, :], axis=1, keepdims=True) * w_a[rows, :]
        l_own = l_own + l_f[rows, :] * w_f[rows, :]
        lane = lax.broadcasted_iota(jnp.int32, (Q, 128), 1)
        stats = jnp.zeros((Q, 128), F32)
        for h in range(hh):
            at = s * R + h * Q
            stats = jnp.where(lane == h, m_own[at:at + Q, :], stats)
            stats = jnp.where(lane == hh + h, l_own[h * Q:(h + 1) * Q, :], stats)
        osend[s, :, hh * vh:] = stats

    def expand(s, g):
        for h in range(g * (hh // ng), (g + 1) * (hh // ng)):
            rows = slice(s * R + h * Q, s * R + (h + 1) * Q)
            a = acc_s[rows, :] * w_a[rows, :] + acc_f[rows, :] * w_f[rows, :]
            high = a.astype(BF16)
            low = (a - high.astype(F32)).astype(BF16)
            both = jnp.dot(
                jnp.concatenate([high, low], axis=0), wv[s, h], preferred_element_type=F32
            )
            osend[s, :, h * vh:(h + 1) * vh] = both[:Q] + both[Q:]

    gcols = (hh // ng) * vh

    def cols_of(g):
        return pl.ds(g * gcols, gcols) if g < ng else pl.ds(hh * vh, 128)

    def ex_copy(s, g):
        n = s * (ng + 1) + g
        return pltpu.make_async_remote_copy(
            src_ref=osend.at[s, :, cols_of(g)], dst_ref=orecv.at[facing[s], :, cols_of(g)],
            send_sem=ex_ss.at[n], recv_sem=ex_rs.at[facing[s] * (ng + 1) + g],
            device_id={"seq": other}, device_id_type=MESH,
        )

    def put(s, g):
        start = halves[s] * (hh * vh) + g * gcols
        if split:
            start = pl.multiple_of(start, 128)
        return pltpu.make_async_copy(
            att.at[s, :, cols_of(g)], att_hbm.at[:, pl.ds(start, gcols)], o_sem.at[s * ng + g]
        )

    finish(own)
    share(0)
    share(1)
    finish(theirs)
    for g in range(ng):
        expand(0, g)
    for s in range(2):
        ex_copy(s, ng).start()
    for g in range(ng):
        ex_copy(0, g).start()
    for g in range(ng):
        expand(1, g)
        ex_copy(1, g).start()

    for s in facing:
        ex_copy(facing[s], ng).wait_recv()
        stats, others = osend[s, :, hh * vh:], orecv[s, :, hh * vh:]
        m_o, m_t = stats[:, :hh], others[:, :hh]
        joint = jnp.maximum(m_o, m_t)
        e_o, e_t = jnp.exp(m_o - joint), jnp.exp(m_t - joint)
        total = e_o * stats[:, hh:2 * hh] + e_t * others[:, hh:2 * hh]
        e_o, e_t = e_o / total, e_t / total
        for g in range(ng):
            ex_copy(facing[s], g).wait_recv()
            for h in range(g * (hh // ng), (g + 1) * (hh // ng)):
                cols = slice(h * vh, (h + 1) * vh)
                start = halves[s] * (hh * vh) + h * vh
                if split:
                    start = pl.multiple_of(start, 128)
                att_ref[:, pl.ds(start, vh)] = (
                    e_o[:, h:h + 1] * osend[s, :, cols] + e_t[:, h:h + 1] * orecv[s, :, cols]
                ).astype(BF16)

    for d in range(1, T):
        ql_copy(d, me).wait_send()
        rs_copy(d, me).wait_send()
        ag_copy(d, me).wait_send()
    if split:
        for i in range(nq):
            qx_copy(i).wait_send()
    for s in range(2):
        for g in range(ng + 1):
            ex_copy(s, g).wait_send()


def hand_over(reb_in, att_in, reb_out, att_out, sems):
    copies = [
        pltpu.make_async_copy(att_in, att_out, sems.at[0]),
        pltpu.make_async_copy(reb_in, reb_out, sems.at[1]),
    ]
    for c in copies:
        c.start()
    for c in copies:
        c.wait()


def body(
    stored_hidden, w_down_kv, kv_gain, evicted_blocks, query_latent, w_up_q,
    w_key_absorb, w_value, query_positions, prefix_lengths, latent_cache,
):
    T = lax.axis_size("tensor")
    rank = kv_gain.shape[0]
    heads, nope = w_key_absorb.shape[:2]
    width = w_down_kv.shape[1]
    rope_dim = width - rank
    Q = query_positions.shape[0]
    requests = prefix_lengths.shape[0]
    half_rows = stored_hidden.shape[1]
    local = half_rows // T
    cache_rows = latent_cache.shape[0]
    bk = min(2048, cache_rows)
    nb = cache_rows // bk
    kt = min(1024, cache_rows)
    ke = min(1024, cache_rows)
    kd = rank + -(-(rope_dim + requests) // 128) * 128
    head_qk = nope + rope_dim
    hh = heads // 2
    split = (hh * head_qk) % 128 == 0
    held = hh if split else heads
    nq = max(1, held // 4)
    ng = max(1, hh // 4)
    vh = w_value.shape[2]
    R = hh * Q
    half = np.arange(rope_dim // 2, dtype=np.float64) * (-2.0 / rope_dim)
    freq = jnp.asarray(np.tile(10000.0 ** half, 2)[None, :].astype(np.float32))
    cfg = (T, nope, rank, rope_dim, Q, requests, split, nq, nb, bk, ng, kt, ke)
    hbm = pl.BlockSpec(memory_space=pl.ANY)
    dma = pltpu.SemaphoreType.DMA
    pieces = 2 * (ng + 1)
    rebuilt = jax.ShapeDtypeStruct((1, local, width), BF16)
    attended = jax.ShapeDtypeStruct((Q, heads * vh), BF16)
    outs = pl.pallas_call(
        functools.partial(kernel, cfg),
        name="rebuild_attend",
        out_shape=(rebuilt, attended),
        in_specs=[hbm] * 12,
        out_specs=(pl.BlockSpec(memory_space=pltpu.VMEM),) * 2,
        scratch_shapes=[
            pltpu.SMEM(evicted_blocks.shape, jnp.int32),
            pltpu.SMEM(query_positions.shape, jnp.int32),
            pltpu.SMEM(prefix_lengths.shape, jnp.int32),
            pltpu.VMEM(freq.shape, F32),
            pltpu.VMEM(kv_gain.shape, BF16),
            pltpu.VMEM((half_rows, w_down_kv.shape[0]), BF16),
            pltpu.VMEM(w_down_kv.shape[::-1], BF16),
            pltpu.VMEM((T,) + query_latent.shape, BF16),
            pltpu.VMEM((Q, query_latent.shape[1]), F32),
            pltpu.VMEM((w_up_q.shape[0], held * head_qk), BF16),
            pltpu.VMEM((held,) + w_key_absorb.shape[1:], BF16),
            pltpu.VMEM((2, hh) + w_value.shape[1:], BF16),
            pltpu.VMEM((kd, cache_rows), BF16),
            pltpu.VMEM((2 * R, kd), BF16),
            pltpu.VMEM((T, local, width), F32),
            pltpu.VMEM((T, local, width), F32),
            pltpu.VMEM((local, width), BF16),
            pltpu.VMEM((T, local, width), BF16),
            pltpu.VMEM((half_rows, kd), BF16),
            pltpu.VMEM((2 * R, cache_rows), F32),
            pltpu.VMEM((2 * R, 1 * ke), BF16),
            pltpu.VMEM((2 * R, 128), F32),
            pltpu.VMEM((2 * R, 128), F32),
            pltpu.VMEM((2 * R, rank), F32),
            pltpu.VMEM((2, Q, hh * vh + 128), F32),
            pltpu.VMEM((2, Q, hh * vh + 128), F32),
            dma((5,)), dma((6,)), dma((nq,)), dma((nb,)),
            dma((T,)), dma((T,)), dma((T,)), dma((T,)), dma((T,)), dma((T,)),
            dma((pieces,)), dma((pieces,)), dma((nq,)), dma((nq,)),
        ],
        compiler_params=pltpu.CompilerParams(
            collective_id=0, has_side_effects=True, vmem_limit_bytes=52000 * 1024
        ),
    )(
        evicted_blocks,
        *(pltpu.with_memory_space_constraint(x, pltpu.HBM) for x in (
            query_positions, prefix_lengths, freq, kv_gain, stored_hidden, w_down_kv.T,
            query_latent, w_up_q, w_key_absorb, w_value, latent_cache.T,
        )),
    )
    return pl.pallas_call(
        hand_over,
        name="hand_over",
        out_shape=(rebuilt, attended),
        in_specs=[hbm] * 2,
        out_specs=(hbm,) * 2,
        scratch_shapes=[dma((2,))],
        compiler_params=pltpu.CompilerParams(vmem_limit_bytes=52000 * 1024),
    )(*outs)


def solution(mesh):
    placed = (
        P(("groups", "seq"), None, "tensor"),
        P("tensor", None),
        P(),
        P("groups"),
        P(("groups", "tensor"), None),
        P(None, "tensor"),
        P("tensor", None, None),
        P("tensor", None, None),
        P("groups"),
        P("groups"),
        P(("groups", "seq"), None),
    )
    return jax.shard_map(
        body,
        mesh=mesh,
        in_specs=placed,
        out_specs=(P(("groups", "seq"), "tensor", None), P("groups", "tensor")),
        check_vma=False,
    )
```

```python
import functools
import numpy as np
import jax
import jax.numpy as jnp
from jax import lax
from jax.experimental import pallas as pl
from jax.experimental.pallas import tpu as pltpu
from jax.sharding import PartitionSpec as P

BLK = 128
NEG = -1e30
FLOOR = -1e20
FAR = 2**30
NORM_EPS = 1e-06
F32 = jnp.float32
BF16 = jnp.bfloat16
MESH = pl.DeviceIdType.MESH


def swap_halves(x):
    half = x.shape[-1] // 2
    return jnp.concatenate([x[:, half:], x[:, :half]], axis=-1)


def trig(pos, freq, rope_dim):
    angle = pos.astype(F32) * freq
    lane = lax.broadcasted_iota(jnp.int32, angle.shape, 1)
    sine = jnp.sin(angle)
    return jnp.cos(angle), jnp.where(lane < rope_dim // 2, -sine, sine)


def kernel(
    cfg,
    eb_hbm, qp_hbm, pf_hbm, freq_hbm, gain_hbm,
    hid_hbm, wd_hbm, ql_hbm, wq_hbm, wk_hbm, wv_hbm, kc_hbm,
    reb_ref, att_ref,
    eb_ref, qp_ref, pf_ref, freq_ref, gain_ref,
    hid, wd, ql, qlf, wq, wk, wv, kc,
    qf, part, rsum, rown, rall, fx, sb, pb, mx_s, l_s, acc_s, osend, orecv,
    i_sem, w_sem, q_sem, c_sem, ql_ss, ql_rs, rs_ss, rs_rs, ag_ss, ag_rs,
    ex_ss, ex_rs, qx_ss, qx_rs,
):
    T, nope, rank, rope_dim, Q, requests, split, nq, nb, bk, ng, kt, ke = cfg
    me = lax.axis_index("tensor")
    sq = lax.axis_index("seq")
    other = 1 - sq
    head_qk = nope + rope_dim
    piece = ql_hbm.shape[0]
    half_rows = hid.shape[0]
    local = half_rows // T
    n_evicted = eb_ref.shape[0]
    hh, vh = wv.shape[1], wv.shape[3]
    hq = wk.shape[0] // nq
    width = rank + rope_dim
    kd, nk = kc.shape
    extra = kd - width
    halves = (sq, other) if split else (0, 1)
    facing = (1, 0) if split else (0, 1)

    def far(d):
        return lax.rem(me + d, T)

    def near(d):
        return lax.rem(me + T - d, T)

    upper = lax.div(2 * me, T)

    def distant(k):
        low = k + lax.div(k + T - me, T)
        high = T - 1 - k - lax.div(me + 1 + k, T)
        return upper * low + (1 - upper) * high

    barrier = pltpu.get_barrier_semaphore()
    for k in range(T - 1):
        pl.semaphore_signal(
            barrier, inc=1, device_id={"tensor": distant(k)}, device_id_type=MESH
        )
    pl.semaphore_signal(barrier, inc=1, device_id={"seq": other}, device_id_type=MESH)

    small = [
        pltpu.make_async_copy(src, dst, i_sem.at[n])
        for n, (src, dst) in enumerate((
            (eb_hbm, eb_ref), (qp_hbm, qp_ref), (pf_hbm, pf_ref),
            (freq_hbm, freq_ref), (gain_hbm, gain_ref),
        ))
    ]
    own_q = pltpu.make_async_copy(ql_hbm, ql.at[me], w_sem.at[0])
    c_hid = pltpu.make_async_copy(hid_hbm.at[0], hid, w_sem.at[1])
    c_wd = pltpu.make_async_copy(wd_hbm, wd, w_sem.at[2])
    wide = hq * head_qk
    first_head = sq * hh if split else 0
    c_wk = pltpu.make_async_copy(wk_hbm.at[pl.ds(first_head, nq * hq)], wk, w_sem.at[3])
    c_wv = [
        pltpu.make_async_copy(wv_hbm.at[pl.ds(halves[s] * hh, hh)], wv.at[s], w_sem.at[4 + s])
        for s in range(2)
    ]

    def c_wq_of(i):
        start = sq * (nq * wide) + i * wide if split else i * wide
        if split:
            start = pl.multiple_of(start, 128)
        return pltpu.make_async_copy(
            wq_hbm.at[:, pl.ds(start, wide)], wq.at[:, pl.ds(i * wide, wide)], q_sem.at[i]
        )

    c_wq = [c_wq_of(i) for i in range(nq)]
    c_kc = [
        pltpu.make_async_copy(
            kc_hbm.at[:, pl.ds(i * bk, bk)], kc.at[pl.ds(0, width), pl.ds(i * bk, bk)],
            c_sem.at[i],
        )
        for i in range(nb)
    ]

    own_q.start()
    for c in small:
        c.start()
    c_hid.start()
    c_wd.start()
    for c in c_wq:
        c.start()
    c_wk.start()
    for c in c_kc:
        c.start()
    for c in c_wv:
        c.start()

    def ql_copy(k):
        return pltpu.make_async_remote_copy(
            src_ref=ql_hbm, dst_ref=ql.at[me], send_sem=ql_ss.at[k], recv_sem=ql_rs.at[me],
            device_id={"tensor": distant(k)}, device_id_type=MESH,
        )

    def ql_from(d):
        return pltpu.make_async_remote_copy(
            src_ref=ql_hbm, dst_ref=ql.at[near(d)], send_sem=ql_ss.at[0],
            recv_sem=ql_rs.at[near(d)], device_id={"tensor": near(d)}, device_id_type=MESH,
        )

    def rs_copy(d, slot):
        return pltpu.make_async_remote_copy(
            src_ref=part.at[far(d)], dst_ref=rsum.at[slot], send_sem=rs_ss.at[d],
            recv_sem=rs_rs.at[d], device_id={"tensor": far(d)}, device_id_type=MESH,
        )

    def qx_copy(i):
        size = hq * Q
        return pltpu.make_async_remote_copy(
            src_ref=qf.at[pl.ds(i * size, size)],
            dst_ref=qf.at[pl.ds((nq + i) * size, size)], send_sem=qx_ss.at[i],
            recv_sem=qx_rs.at[i], device_id={"seq": other}, device_id_type=MESH,
        )

    def ag_copy(d, slot):
        return pltpu.make_async_remote_copy(
            src_ref=rown, dst_ref=rall.at[slot], send_sem=ag_ss.at[d], recv_sem=ag_rs.at[d],
            device_id={"tensor": far(d)}, device_id_type=MESH,
        )

    pl.semaphore_wait(barrier, T)
    for k in range(T - 1):
        ql_copy(k).start()

    for c in small:
        c.wait()
    freq = freq_ref[...]
    qrow = lax.broadcasted_iota(jnp.int32, (Q, 1), 0)
    qpos = lax.fori_loop(
        0, Q, lambda i, v: jnp.where(qrow == i, qp_ref[i], v), jnp.zeros((Q, 1), jnp.int32)
    )
    qcos, qsin = trig(qpos, freq, rope_dim)
    per = Q // requests
    belongs = lax.broadcasted_iota(jnp.int32, (Q, extra), 0) // per
    chosen = jnp.where(
        belongs == lax.broadcasted_iota(jnp.int32, (Q, extra), 1), 1.0, 0.0
    )
    flat0 = sq * half_rows + me * local
    rpos = (
        eb_ref[flat0 // BLK] * BLK + flat0 % BLK
        + lax.broadcasted_iota(jnp.int32, (local, 1), 0)
    )
    rcos, rsin = trig(rpos, freq, rope_dim)

    def limits(axis, shape):
        index = lax.broadcasted_iota(jnp.int32, shape, axis)
        limit = jnp.full(shape, FAR, jnp.int32)
        for r in range(requests):
            limit = jnp.where(index == r, pf_ref[r], limit)
        return jnp.where(index < requests, limit, 2 * (FAR - 1) + 1)

    pos = sq * nk + lax.broadcasted_iota(jnp.int32, (1, nk), 1)
    eff = pos
    for e in range(n_evicted):
        first = eb_ref[e] * BLK
        eff = jnp.where((pos >= first) & (pos < first + BLK), FAR, eff)
    kc[width:, :] = jnp.where(eff < limits(0, (extra, 1)), 0.0, NEG).astype(BF16)

    flat = sq * half_rows + lax.broadcasted_iota(jnp.int32, (half_rows, 1), 0)
    fpos = flat
    for e in range(n_evicted):
        inside = (flat >= e * BLK) & (flat < (e + 1) * BLK)
        fpos = jnp.where(inside, eb_ref[e] * BLK + flat - e * BLK, fpos)
    fbias = jnp.where(fpos < limits(1, (1, extra)), 0.0, NEG)

    c_hid.wait()
    c_wd.wait()
    partial = lax.dot_general(
        hid[...], wd[...], (((1,), (1,)), ((), ())), preferred_element_type=F32
    )
    for t in range(T):
        part[t] = partial[t * local:(t + 1) * local, :]
    rsum[me] = part[me]
    for d in range(1, T):
        rs_copy(d, me).start()

    own_q.wait()
    for c in c_wq:
        c.wait()
    c_wk.wait()
    for d in range(1, T):
        ql_from(d).wait_recv()
    for t in range(T):
        qlf[t * piece:(t + 1) * piece, :] = ql[t].astype(F32)
    queries = qlf[...].astype(BF16)
    scale = float(head_qk) ** (-0.5)

    def project(i):
        return jnp.dot(
            queries, wq[:, i * wide:(i + 1) * wide], preferred_element_type=F32
        )

    def absorb(i, proj):
        for j in range(hq):
            slot, h = divmod(i * hq + j, hh)
            at = slot * hh * Q + h * Q
            rows = slice(at, at + Q)
            q_nope = proj[:, j * head_qk:j * head_qk + nope].astype(BF16)
            q_rope = proj[:, j * head_qk + nope:(j + 1) * head_qk]
            absorbed = jnp.dot(q_nope, wk[i * hq + j], preferred_element_type=F32)
            qf[rows, :rank] = (absorbed * scale).astype(BF16)
            turned = q_rope * qcos + swap_halves(q_rope) * qsin
            qf[rows, rank:] = jnp.concatenate(
                [turned * scale, chosen], axis=-1
            ).astype(BF16)

    ahead = project(0)
    for i in range(1, nq):
        later = project(i)
        absorb(i - 1, ahead)
        ahead = later
        if split:
            qx_copy(i - 1).start()
    absorb(nq - 1, ahead)
    if split:
        qx_copy(nq - 1).start()

    for c in c_kc:
        c.wait()
    nt, ne = nk // kt, nk // ke
    LANES = 128

    def fold(op, x):
        parts = [x[:, c * LANES:(c + 1) * LANES] for c in range(x.shape[1] // LANES)]
        while len(parts) > 1:
            parts = [
                op(parts[n], parts[n + 1]) if n + 1 < len(parts) else parts[n]
                for n in range(0, len(parts), 2)
            ]
        return parts[0]

    R = hh * Q
    own, theirs, both = slice(0, R), slice(R, 2 * R), slice(0, 2 * R)

    def score(rows, t):
        cols = slice(t * kt, (t + 1) * kt)
        dots = jnp.dot(qf[rows, :], kc[:, cols], preferred_element_type=F32)
        sb[rows, cols] = dots
        top = fold(jnp.maximum, dots)
        mx_s[rows, :] = top if t == 0 else jnp.maximum(mx_s[rows, :], top)

    def highest(rows):
        top = jnp.maximum(jnp.max(mx_s[rows, :], axis=1, keepdims=True), FLOOR)
        mx_s[rows, :] = jnp.broadcast_to(top, mx_s[rows, :].shape)
        return top

    def weigh(rows, t):
        cols = slice(t * ke, (t + 1) * ke)
        top = mx_s[rows, :]
        ps = [jnp.exp(sb[rows, c:c + LANES] - top) for c in range(t * ke, (t + 1) * ke, LANES)]
        p = jnp.concatenate(ps, axis=-1)
        total = fold(jnp.add, p)
        l_s[rows, :] = total if t == 0 else l_s[rows, :] + total
        out = lax.dot_general(
            p.astype(BF16), kc[:rank, cols], (((1,), (1,)), ((), ())),
            preferred_element_type=F32,
        )
        acc_s[rows, :] = out if t == 0 else acc_s[rows, :] + out

    def ahead_of(rows, t):
        cols = slice(t * ke, (t + 1) * ke)
        top = mx_s[rows, :]
        ps = [jnp.exp(sb[rows, c:c + LANES] - top) for c in range(t * ke, (t + 1) * ke, LANES)]
        p = jnp.concatenate(ps, axis=-1)
        total = fold(jnp.add, p)
        l_s[rows, :] = total if t == 0 else l_s[rows, :] + total
        pb[rows, :] = p.astype(BF16)

    def finish(rows, t):
        out = lax.dot_general(
            pb[rows, :], kc[:rank, t * ke:(t + 1) * ke], (((1,), (1,)), ((), ())),
            preferred_element_type=F32,
        )
        acc_s[rows, :] = out if t == 0 else acc_s[rows, :] + out

    lead, some = max(1, 6 * nt // 8), max(1, 3 * nt // 8)
    for t in range(lead):
        score(own, t)
    if split:
        for i in range(nq):
            qx_copy(i).wait_recv()
    for t in range(some):
        score(theirs, t)

    for d in range(1, T):
        rs_copy(d, near(d)).wait_recv()
    summed = rsum[0]
    for t in range(1, T):
        summed = summed + rsum[t]
    latent = summed[:, :rank]
    mean_square = jnp.mean(latent * latent, axis=-1, keepdims=True)
    normed = latent / jnp.sqrt(mean_square + NORM_EPS) * gain_ref[...].astype(F32).reshape(1, rank)
    tail = summed[:, rank:]
    turned = tail * rcos + swap_halves(tail) * rsin
    rown[:, :rank] = normed.astype(BF16)
    rown[:, rank:] = turned.astype(BF16)
    rall[me] = rown[...]
    for d in range(1, T):
        ag_copy(d, me).start()
    reb_ref[0] = rown[...]

    for t in range(lead, nt):
        score(own, t)
    for t in range(some, nt):
        score(theirs, t)
    m_a = jnp.concatenate([highest(own), highest(theirs)], axis=0)
    first = 1 if ne > 2 else 0
    for t in range(first):
        weigh(both, t)
    if ne > 1:
        ahead_of(both, first)
    c_wv[0].wait()
    if ne > 1:
        finish(both, first)
    for t in range(first + 1, ne - 1):
        weigh(both, t)
    ahead_of(both, ne - 1)

    for d in range(1, T):
        ag_copy(d, near(d)).wait_recv()
    c_wv[1].wait()
    fresh = jnp.concatenate([rall[t].astype(F32) for t in range(T)], axis=0)
    fx[:, :rank] = fresh[:, :rank].astype(BF16)
    fx[:, rank:] = jnp.concatenate([fresh[:, rank:], fbias], axis=-1).astype(BF16)

    s_f = lax.dot_general(
        qf[...], fx[...], (((1,), (1,)), ((), ())), preferred_element_type=F32
    )
    m_f = jnp.maximum(jnp.max(s_f, axis=1, keepdims=True), FLOOR)
    p_f = jnp.exp(s_f - m_f)
    l_f = jnp.sum(p_f, axis=1, keepdims=True)
    acc_f = jnp.dot(p_f.astype(BF16), fx[:, :rank], preferred_element_type=F32)
    m_own = jnp.maximum(m_a, m_f)
    w_a, w_f = jnp.exp(m_a - m_own), jnp.exp(m_f - m_own)

    def share(s):
        rows = slice(s * R, (s + 1) * R)
        l_own = jnp.sum(l_s[rows, :], axis=1, keepdims=True) * w_a[rows, :]
        l_own = l_own + l_f[rows, :] * w_f[rows, :]
        lane = lax.broadcasted_iota(jnp.int32, (Q, 128), 1)
        stats = jnp.zeros((Q, 128), F32)
        for h in range(hh):
            at = s * R + h * Q
            stats = jnp.where(lane == h, m_own[at:at + Q, :], stats)
            stats = jnp.where(lane == hh + h, l_own[h * Q:(h + 1) * Q, :], stats)
        osend[s, :, hh * vh:] = stats

    def expand(s, g):
        for h in range(g * (hh // ng), (g + 1) * (hh // ng)):
            rows = slice(s * R + h * Q, s * R + (h + 1) * Q)
            a = acc_s[rows, :] * w_a[rows, :] + acc_f[rows, :] * w_f[rows, :]
            high = a.astype(BF16)
            low = (a - high.astype(F32)).astype(BF16)
            both = jnp.dot(
                jnp.concatenate([high, low], axis=0), wv[s, h], preferred_element_type=F32
            )
            osend[s, :, h * vh:(h + 1) * vh] = both[:Q] + both[Q:]

    gcols = (hh // ng) * vh

    def cols_of(g):
        return pl.ds(g * gcols, gcols) if g < ng else pl.ds(hh * vh, 128)

    def ex_copy(s, g):
        n = s * (ng + 1) + g
        return pltpu.make_async_remote_copy(
            src_ref=osend.at[s, :, cols_of(g)], dst_ref=orecv.at[facing[s], :, cols_of(g)],
            send_sem=ex_ss.at[n], recv_sem=ex_rs.at[facing[s] * (ng + 1) + g],
            device_id={"seq": other}, device_id_type=MESH,
        )

    s_f = lax.dot_general(
        qf[...], fx[...], (((1,), (1,)), ((), ())), preferred_element_type=F32
    )
    m_f = jnp.maximum(jnp.max(s_f, axis=1, keepdims=True), FLOOR)
    p_f = jnp.exp(s_f - m_f)
    l_f = jnp.sum(p_f, axis=1, keepdims=True)
    acc_f = jnp.dot(p_f.astype(BF16), fx[:, :rank], preferred_element_type=F32)
    m_own = jnp.maximum(m_a, m_f)
    w_a, w_f = jnp.exp(m_a - m_own), jnp.exp(m_f - m_own)

    def share(s):
        rows = slice(s * R, (s + 1) * R)
        l_own = jnp.sum(l_s[rows, :], axis=1, keepdims=True) * w_a[rows, :]
        l_own = l_own + l_f[rows, :] * w_f[rows, :]
        lane = lax.broadcasted_iota(jnp.int32, (Q, 128), 1)
        stats = jnp.zeros((Q, 128), F32)
        for h in range(hh):
            at = s * R + h * Q
            stats = jnp.where(lane == h, m_own[at:at + Q, :], stats)
            stats = jnp.where(lane == hh + h, l_own[h * Q:(h + 1) * Q, :], stats)
        osend[s, :, hh * vh:] = stats

    def expand(s, g):
        for h in range(g * (hh // ng), (g + 1) * (hh // ng)):
            rows = slice(s * R + h * Q, s * R + (h + 1) * Q)
            a = acc_s[rows, :] * w_a[rows, :] + acc_f[rows, :] * w_f[rows, :]
            high = a.astype(BF16)
            low = (a - high.astype(F32)).astype(BF16)
            both = jnp.dot(
                jnp.concatenate([high, low], axis=0), wv[s, h], preferred_element_type=F32
            )
            osend[s, :, h * vh:(h + 1) * vh] = both[:Q] + both[Q:]

    gcols = (hh // ng) * vh

    def cols_of(g):
        return pl.ds(g * gcols, gcols) if g < ng else pl.ds(hh * vh, 128)

    def ex_copy(s, g):
        n = s * (ng + 1) + g
        return pltpu.make_async_remote_copy(
            src_ref=osend.at[s, :, cols_of(g)], dst_ref=orecv.at[facing[s], :, cols_of(g)],
            send_sem=ex_ss.at[n], recv_sem=ex_rs.at[facing[s] * (ng + 1) + g],
            device_id={"seq": other}, device_id_type=MESH,
        )

    def put(s, g):
        start = halves[s] * (hh * vh) + g * gcols
        if split:
            start = pl.multiple_of(start, 128)
        return pltpu.make_async_copy(
            att.at[s, :, cols_of(g)], att_hbm.at[:, pl.ds(start, gcols)], o_sem.at[s * ng + g]
        )

    finish(own, ne - 1)
    share(0)
    share(1)
    finish(theirs, ne - 1)
    for g in range(ng):
        expand(0, g)
    for s in range(2):
        ex_copy(s, ng).start()
    for g in range(ng):
        ex_copy(0, g).start()
    for g in range(ng):
        expand(1, g)
        ex_copy(1, g).start()

    for s in range(2):
        ex_copy(s, ng).wait_recv()
    weights = []
    for s in range(2):
        stats, others = osend[s, :, hh * vh:], orecv[s, :, hh * vh:]
        m_o, m_t = stats[:, :hh], others[:, :hh]
        joint = jnp.maximum(m_o, m_t)
        e_o, e_t = jnp.exp(m_o - joint), jnp.exp(m_t - joint)
        total = e_o * stats[:, hh:2 * hh] + e_t * others[:, hh:2 * hh]
        weights.append((e_o / total, e_t / total))
    for s in facing:
        e_o, e_t = weights[s]
        for g in range(ng):
            ex_copy(facing[s], g).wait_recv()
        for h in range(hh):
            cols = slice(h * vh, (h + 1) * vh)
            start = halves[s] * (hh * vh) + h * vh
            if split:
                start = pl.multiple_of(start, 128)
            att_ref[:, pl.ds(start, vh)] = (
                e_o[:, h:h + 1] * osend[s, :, cols] + e_t[:, h:h + 1] * orecv[s, :, cols]
            ).astype(BF16)

    for d in range(1, T):
        ql_copy(d - 1).wait_send()
        rs_copy(d, me).wait_send()
        ag_copy(d, me).wait_send()
    if split:
        for i in range(nq):
            qx_copy(i).wait_send()
    for s in range(2):
        for g in range(ng + 1):
            ex_copy(s, g).wait_send()


def hand_over(reb_in, att_in, reb_out, att_out, sems):
    copies = [
        pltpu.make_async_copy(att_in, att_out, sems.at[0]),
        pltpu.make_async_copy(reb_in, reb_out, sems.at[1]),
    ]
    for c in copies:
        c.start()
    for c in copies:
        c.wait()


def body(
    stored_hidden, w_down_kv, kv_gain, evicted_blocks, query_latent, w_up_q,
    w_key_absorb, w_value, query_positions, prefix_lengths, latent_cache,
):
    T = lax.axis_size("tensor")
    rank = kv_gain.shape[0]
    heads, nope = w_key_absorb.shape[:2]
    width = w_down_kv.shape[1]
    rope_dim = width - rank
    Q = query_positions.shape[0]
    requests = prefix_lengths.shape[0]
    half_rows = stored_hidden.shape[1]
    local = half_rows // T
    cache_rows = latent_cache.shape[0]
    bk = min(2048, cache_rows)
    nb = cache_rows // bk
    kt = min(1024, cache_rows)
    ke = min(1024, cache_rows)
    kd = rank + -(-(rope_dim + requests) // 128) * 128
    head_qk = nope + rope_dim
    hh = heads // 2
    split = (hh * head_qk) % 128 == 0
    held = hh if split else heads
    nq = max(1, held // 4)
    ng = max(1, hh // 4)
    vh = w_value.shape[2]
    R = hh * Q
    half = np.arange(rope_dim // 2, dtype=np.float64) * (-2.0 / rope_dim)
    freq = jnp.asarray(np.tile(10000.0 ** half, 2)[None, :].astype(np.float32))
    cfg = (T, nope, rank, rope_dim, Q, requests, split, nq, nb, bk, ng, kt, ke)
    hbm = pl.BlockSpec(memory_space=pl.ANY)
    dma = pltpu.SemaphoreType.DMA
    pieces = 2 * (ng + 1)
    rebuilt = jax.ShapeDtypeStruct((1, local, width), BF16)
    attended = jax.ShapeDtypeStruct((Q, heads * vh), BF16)
    outs = pl.pallas_call(
        functools.partial(kernel, cfg),
        name="rebuild_attend",
        out_shape=(rebuilt, attended),
        in_specs=[hbm] * 12,
        out_specs=(pl.BlockSpec(memory_space=pltpu.VMEM),) * 2,
        scratch_shapes=[
            pltpu.SMEM(evicted_blocks.shape, jnp.int32),
            pltpu.SMEM(query_positions.shape, jnp.int32),
            pltpu.SMEM(prefix_lengths.shape, jnp.int32),
            pltpu.VMEM(freq.shape, F32),
            pltpu.VMEM(kv_gain.shape, BF16),
            pltpu.VMEM((half_rows, w_down_kv.shape[0]), BF16),
            pltpu.VMEM(w_down_kv.shape[::-1], BF16),
            pltpu.VMEM((T,) + query_latent.shape, BF16),
            pltpu.VMEM((Q, query_latent.shape[1]), F32),
            pltpu.VMEM((w_up_q.shape[0], held * head_qk), BF16),
            pltpu.VMEM((held,) + w_key_absorb.shape[1:], BF16),
            pltpu.VMEM((2, hh) + w_value.shape[1:], BF16),
            pltpu.VMEM((kd, cache_rows), BF16),
            pltpu.VMEM((2 * R, kd), BF16),
            pltpu.VMEM((T, local, width), F32),
            pltpu.VMEM((T, local, width), F32),
            pltpu.VMEM((local, width), BF16),
            pltpu.VMEM((T, local, width), BF16),
            pltpu.VMEM((half_rows, kd), BF16),
            pltpu.VMEM((2 * R, cache_rows), F32),
            pltpu.VMEM((2 * R, 1 * ke), BF16),
            pltpu.VMEM((2 * R, 128), F32),
            pltpu.VMEM((2 * R, 128), F32),
            pltpu.VMEM((2 * R, rank), F32),
            pltpu.VMEM((2, Q, hh * vh + 128), F32),
            pltpu.VMEM((2, Q, hh * vh + 128), F32),
            dma((5,)), dma((6,)), dma((nq,)), dma((nb,)),
            dma((T,)), dma((T,)), dma((T,)), dma((T,)), dma((T,)), dma((T,)),
            dma((pieces,)), dma((pieces,)), dma((nq,)), dma((nq,)),
        ],
        compiler_params=pltpu.CompilerParams(
            collective_id=0, has_side_effects=True, vmem_limit_bytes=52000 * 1024
        ),
    )(
        evicted_blocks,
        *(pltpu.with_memory_space_constraint(x, pltpu.HBM) for x in (
            query_positions, prefix_lengths, freq, kv_gain, stored_hidden, w_down_kv.T,
            query_latent, w_up_q, w_key_absorb, w_value, latent_cache.T,
        )),
    )
    return pl.pallas_call(
        hand_over,
        name="hand_over",
        out_shape=(rebuilt, attended),
        in_specs=[hbm] * 2,
        out_specs=(hbm,) * 2,
        scratch_shapes=[dma((2,))],
        compiler_params=pltpu.CompilerParams(vmem_limit_bytes=52000 * 1024),
    )(*outs)


def solution(mesh):
    placed = (
        P(("groups", "seq"), None, "tensor"),
        P("tensor", None),
        P(),
        P("groups"),
        P(("groups", "tensor"), None),
        P(None, "tensor"),
        P("tensor", None, None),
        P("tensor", None, None),
        P("groups"),
        P("groups"),
        P(("groups", "seq"), None),
    )
    return jax.shard_map(
        body,
        mesh=mesh,
        in_specs=placed,
        out_specs=(P(("groups", "seq"), "tensor", None), P("groups", "tensor")),
        check_vma=False,
    )
```

```python
import functools
import numpy as np
import jax
import jax.numpy as jnp
from jax import lax
from jax.experimental import pallas as pl
from jax.experimental.pallas import tpu as pltpu
from jax.sharding import PartitionSpec as P

BLK = 128
NEG = -1e30
FLOOR = -1e20
FAR = 2**30
NORM_EPS = 1e-06
F32 = jnp.float32
BF16 = jnp.bfloat16
MESH = pl.DeviceIdType.MESH


def swap_halves(x):
    half = x.shape[-1] // 2
    return jnp.concatenate([x[:, half:], x[:, :half]], axis=-1)


def trig(pos, freq, rope_dim):
    angle = pos.astype(F32) * freq
    lane = lax.broadcasted_iota(jnp.int32, angle.shape, 1)
    sine = jnp.sin(angle)
    return jnp.cos(angle), jnp.where(lane < rope_dim // 2, -sine, sine)


def kernel(
    cfg,
    eb_hbm, qp_hbm, pf_hbm, freq_hbm, gain_hbm,
    hid_hbm, wd_hbm, ql_hbm, wq_hbm, wk_hbm, wv_hbm, kc_hbm,
    reb_ref, att_ref,
    eb_ref, qp_ref, pf_ref, freq_ref, gain_ref,
    hid, wd, ql, qlf, wq, wk, wv, kc,
    qf, part, rsum, rown, rall, fx, sb, pb, mx_s, l_s, acc_s, osend, orecv,
    i_sem, w_sem, q_sem, c_sem, ql_ss, ql_rs, rs_ss, rs_rs, ag_ss, ag_rs,
    ex_ss, ex_rs, qx_ss, qx_rs,
):
    T, nope, rank, rope_dim, Q, requests, split, nq, nb, bk, ng, kt, ke = cfg
    me = lax.axis_index("tensor")
    sq = lax.axis_index("seq")
    other = 1 - sq
    head_qk = nope + rope_dim
    piece = ql_hbm.shape[0]
    half_rows = hid.shape[0]
    local = half_rows // T
    n_evicted = eb_ref.shape[0]
    hh, vh = wv.shape[1], wv.shape[3]
    hq = wk.shape[0] // nq
    width = rank + rope_dim
    kd, nk = kc.shape
    extra = kd - width
    halves = (sq, other) if split else (0, 1)
    facing = (1, 0) if split else (0, 1)

    def far(d):
        return lax.rem(me + d, T)

    def settle(ref, sem):
        pltpu.make_async_copy(ref, ref, sem).wait()

    upper = lax.div(2 * me, T)

    def distant(k):
        low = k + lax.div(k + T - me, T)
        high = T - 1 - k - lax.div(me + 1 + k, T)
        return upper * low + (1 - upper) * high

    barrier = pltpu.get_barrier_semaphore()
    for k in range(T - 1):
        pl.semaphore_signal(
            barrier, inc=1, device_id={"tensor": distant(k)}, device_id_type=MESH
        )
    pl.semaphore_signal(barrier, inc=1, device_id={"seq": other}, device_id_type=MESH)

    small = [
        pltpu.make_async_copy(src, dst, i_sem.at[n])
        for n, (src, dst) in enumerate((
            (eb_hbm, eb_ref), (qp_hbm, qp_ref), (pf_hbm, pf_ref),
            (freq_hbm, freq_ref), (gain_hbm, gain_ref),
        ))
    ]
    own_q = pltpu.make_async_copy(ql_hbm, ql.at[me], w_sem.at[0])
    c_hid = pltpu.make_async_copy(hid_hbm.at[0], hid, w_sem.at[1])
    c_wd = pltpu.make_async_copy(wd_hbm, wd, w_sem.at[2])
    wide = hq * head_qk
    first_head = sq * hh if split else 0
    c_wk = pltpu.make_async_copy(wk_hbm.at[pl.ds(first_head, nq * hq)], wk, w_sem.at[3])
    c_wv = [
        pltpu.make_async_copy(wv_hbm.at[pl.ds(halves[s] * hh, hh)], wv.at[s], w_sem.at[4 + s])
        for s in range(2)
    ]

    def c_wq_of(i):
        start = sq * (nq * wide) + i * wide if split else i * wide
        if split:
            start = pl.multiple_of(start, 128)
        return pltpu.make_async_copy(
            wq_hbm.at[:, pl.ds(start, wide)], wq.at[:, pl.ds(i * wide, wide)], q_sem
        )

    c_wq = [c_wq_of(i) for i in range(nq)]
    c_kc = [
        pltpu.make_async_copy(
            kc_hbm.at[:, pl.ds(i * bk, bk)], kc.at[pl.ds(0, width), pl.ds(i * bk, bk)],
            c_sem,
        )
        for i in range(nb)
    ]

    own_q.start()
    for c in small:
        c.start()
    c_hid.start()
    c_wd.start()
    for c in c_wq:
        c.start()
    c_wk.start()
    for c in c_kc:
        c.start()
    for c in c_wv:
        c.start()

    def ql_copy(k):
        return pltpu.make_async_remote_copy(
            src_ref=ql_hbm, dst_ref=ql.at[me], send_sem=ql_ss, recv_sem=ql_rs,
            device_id={"tensor": distant(k)}, device_id_type=MESH,
        )

    def rs_copy(d, slot):
        return pltpu.make_async_remote_copy(
            src_ref=part.at[far(d)], dst_ref=rsum.at[slot], send_sem=rs_ss,
            recv_sem=rs_rs, device_id={"tensor": far(d)}, device_id_type=MESH,
        )

    def qx_copy(i):
        size = hq * Q
        return pltpu.make_async_remote_copy(
            src_ref=qf.at[pl.ds(i * size, size)],
            dst_ref=qf.at[pl.ds((nq + i) * size, size)], send_sem=qx_ss.at[i],
            recv_sem=qx_rs.at[i], device_id={"seq": other}, device_id_type=MESH,
        )

    def ag_copy(d, slot):
        return pltpu.make_async_remote_copy(
            src_ref=rown, dst_ref=rall.at[slot], send_sem=ag_ss, recv_sem=ag_rs,
            device_id={"tensor": far(d)}, device_id_type=MESH,
        )

    pl.semaphore_wait(barrier, T)
    for k in range(T - 1):
        ql_copy(k).start()

    for c in small:
        c.wait()
    freq = freq_ref[...]
    qrow = lax.broadcasted_iota(jnp.int32, (Q, 1), 0)
    qpos = lax.fori_loop(
        0, Q, lambda i, v: jnp.where(qrow == i, qp_ref[i], v), jnp.zeros((Q, 1), jnp.int32)
    )
    qcos, qsin = trig(qpos, freq, rope_dim)
    per = Q // requests
    belongs = lax.broadcasted_iota(jnp.int32, (Q, extra), 0) // per
    chosen = jnp.where(
        belongs == lax.broadcasted_iota(jnp.int32, (Q, extra), 1), 1.0, 0.0
    )
    flat0 = sq * half_rows + me * local
    rpos = (
        eb_ref[flat0 // BLK] * BLK + flat0 % BLK
        + lax.broadcasted_iota(jnp.int32, (local, 1), 0)
    )
    rcos, rsin = trig(rpos, freq, rope_dim)

    def limits(axis, shape):
        index = lax.broadcasted_iota(jnp.int32, shape, axis)
        limit = jnp.full(shape, FAR, jnp.int32)
        for r in range(requests):
            limit = jnp.where(index == r, pf_ref[r], limit)
        return jnp.where(index < requests, limit, 2 * (FAR - 1) + 1)

    pos = sq * nk + lax.broadcasted_iota(jnp.int32, (1, nk), 1)
    eff = pos
    for e in range(n_evicted):
        first = eb_ref[e] * BLK
        eff = jnp.where((pos >= first) & (pos < first + BLK), FAR, eff)
    kc[width:, :] = jnp.where(eff < limits(0, (extra, 1)), 0.0, NEG).astype(BF16)

    flat = sq * half_rows + lax.broadcasted_iota(jnp.int32, (half_rows, 1), 0)
    fpos = flat
    for e in range(n_evicted):
        inside = (flat >= e * BLK) & (flat < (e + 1) * BLK)
        fpos = jnp.where(inside, eb_ref[e] * BLK + flat - e * BLK, fpos)
    fbias = jnp.where(fpos < limits(1, (1, extra)), 0.0, NEG)

    c_hid.wait()
    c_wd.wait()
    partial = lax.dot_general(
        hid[...], wd[...], (((1,), (1,)), ((), ())), preferred_element_type=F32
    )
    for t in range(T):
        part[t] = partial[t * local:(t + 1) * local, :]
    rsum[me] = part[me]
    for d in range(1, T):
        rs_copy(d, me).start()

    own_q.wait()
    settle(wq, q_sem)
    c_wk.wait()
    settle(ql.at[pl.ds(0, T - 1)], ql_rs)
    for t in range(T):
        qlf[t * piece:(t + 1) * piece, :] = ql[t].astype(F32)
    queries = qlf[...].astype(BF16)
    scale = float(head_qk) ** (-0.5)

    def project(i):
        return jnp.dot(
            queries, wq[:, i * wide:(i + 1) * wide], preferred_element_type=F32
        )

    def absorb(i, proj):
        for j in range(hq):
            slot, h = divmod(i * hq + j, hh)
            at = slot * hh * Q + h * Q
            rows = slice(at, at + Q)
            q_nope = proj[:, j * head_qk:j * head_qk + nope].astype(BF16)
            q_rope = proj[:, j * head_qk + nope:(j + 1) * head_qk]
            absorbed = jnp.dot(q_nope, wk[i * hq + j], preferred_element_type=F32)
            qf[rows, :rank] = (absorbed * scale).astype(BF16)
            turned = q_rope * qcos + swap_halves(q_rope) * qsin
            qf[rows, rank:] = jnp.concatenate(
                [turned * scale, chosen], axis=-1
            ).astype(BF16)

    ahead = project(0)
    for i in range(1, nq):
        later = project(i)
        absorb(i - 1, ahead)
        ahead = later
        if split:
            qx_copy(i - 1).start()
    absorb(nq - 1, ahead)
    if split:
        qx_copy(nq - 1).start()

    settle(kc.at[pl.ds(0, width)], c_sem)
    nt, ne = nk // kt, nk // ke
    LANES = 128

    def fold(op, x):
        parts = [x[:, c * LANES:(c + 1) * LANES] for c in range(x.shape[1] // LANES)]
        while len(parts) > 1:
            parts = [
                op(parts[n], parts[n + 1]) if n + 1 < len(parts) else parts[n]
                for n in range(0, len(parts), 2)
            ]
        return parts[0]

    R = hh * Q
    own, theirs, both = slice(0, R), slice(R, 2 * R), slice(0, 2 * R)

    def score(rows, t):
        cols = slice(t * kt, (t + 1) * kt)
        dots = jnp.dot(qf[rows, :], kc[:, cols], preferred_element_type=F32)
        sb[rows, cols] = dots
        top = fold(jnp.maximum, dots)
        mx_s[rows, :] = top if t == 0 else jnp.maximum(mx_s[rows, :], top)

    def highest(rows):
        top = jnp.maximum(jnp.max(mx_s[rows, :], axis=1, keepdims=True), FLOOR)
        mx_s[rows, :] = jnp.broadcast_to(top, mx_s[rows, :].shape)
        return top

    def weigh(rows, t):
        cols = slice(t * ke, (t + 1) * ke)
        top = mx_s[rows, :]
        ps = [jnp.exp(sb[rows, c:c + LANES] - top) for c in range(t * ke, (t + 1) * ke, LANES)]
        p = jnp.concatenate(ps, axis=-1)
        total = fold(jnp.add, p)
        l_s[rows, :] = total if t == 0 else l_s[rows, :] + total
        out = lax.dot_general(
            p.astype(BF16), kc[:rank, cols], (((1,), (1,)), ((), ())),
            preferred_element_type=F32,
        )
        acc_s[rows, :] = out if t == 0 else acc_s[rows, :] + out

    def ahead_of(rows, t):
        cols = slice(t * ke, (t + 1) * ke)
        top = mx_s[rows, :]
        ps = [jnp.exp(sb[rows, c:c + LANES] - top) for c in range(t * ke, (t + 1) * ke, LANES)]
        p = jnp.concatenate(ps, axis=-1)
        total = fold(jnp.add, p)
        l_s[rows, :] = total if t == 0 else l_s[rows, :] + total
        pb[rows, :] = p.astype(BF16)

    def finish(rows, t):
        out = lax.dot_general(
            pb[rows, :], kc[:rank, t * ke:(t + 1) * ke], (((1,), (1,)), ((), ())),
            preferred_element_type=F32,
        )
        acc_s[rows, :] = out if t == 0 else acc_s[rows, :] + out

    lead, some = max(1, 6 * nt // 8), max(1, 3 * nt // 8)
    for t in range(lead):
        score(own, t)
    if split:
        for i in range(nq):
            qx_copy(i).wait_recv()
    for t in range(some):
        score(theirs, t)

    settle(rsum.at[pl.ds(0, T - 1)], rs_rs)
    summed = rsum[0]
    for t in range(1, T):
        summed = summed + rsum[t]
    latent = summed[:, :rank]
    mean_square = jnp.mean(latent * latent, axis=-1, keepdims=True)
    normed = latent / jnp.sqrt(mean_square + NORM_EPS) * gain_ref[...].astype(F32).reshape(1, rank)
    tail = summed[:, rank:]
    turned = tail * rcos + swap_halves(tail) * rsin
    rown[:, :rank] = normed.astype(BF16)
    rown[:, rank:] = turned.astype(BF16)
    rall[me] = rown[...]
    for d in range(1, T):
        ag_copy(d, me).start()
    reb_ref[0] = rown[...]

    for t in range(lead, nt):
        score(own, t)
    for t in range(some, nt):
        score(theirs, t)
    m_a = jnp.concatenate([highest(own), highest(theirs)], axis=0)
    first = 1 if ne > 2 else 0
    for t in range(first):
        weigh(both, t)
    if ne > 1:
        ahead_of(both, first)
    c_wv[0].wait()
    if ne > 1:
        finish(both, first)
    for t in range(first + 1, ne - 1):
        weigh(both, t)
    ahead_of(both, ne - 1)

    settle(rall.at[pl.ds(0, T - 1)], ag_rs)
    c_wv[1].wait()
    fresh = jnp.concatenate([rall[t].astype(F32) for t in range(T)], axis=0)
    fx[:, :rank] = fresh[:, :rank].astype(BF16)
    fx[:, rank:] = jnp.concatenate([fresh[:, rank:], fbias], axis=-1).astype(BF16)

    s_f = lax.dot_general(
        qf[...], fx[...], (((1,), (1,)), ((), ())), preferred_element_type=F32
    )
    m_f = jnp.maximum(jnp.max(s_f, axis=1, keepdims=True), FLOOR)
    p_f = jnp.exp(s_f - m_f)
    l_f = jnp.sum(p_f, axis=1, keepdims=True)
    acc_f = jnp.dot(p_f.astype(BF16), fx[:, :rank], preferred_element_type=F32)
    m_own = jnp.maximum(m_a, m_f)
    w_a, w_f = jnp.exp(m_a - m_own), jnp.exp(m_f - m_own)

    def share(s):
        rows = slice(s * R, (s + 1) * R)
        l_own = jnp.sum(l_s[rows, :], axis=1, keepdims=True) * w_a[rows, :]
        l_own = l_own + l_f[rows, :] * w_f[rows, :]
        lane = lax.broadcasted_iota(jnp.int32, (Q, 128), 1)
        stats = jnp.zeros((Q, 128), F32)
        for h in range(hh):
            at = s * R + h * Q
            stats = jnp.where(lane == h, m_own[at:at + Q, :], stats)
            stats = jnp.where(lane == hh + h, l_own[h * Q:(h + 1) * Q, :], stats)
        osend[s, :, hh * vh:] = stats

    def expand(s, g):
        for h in range(g * (hh // ng), (g + 1) * (hh // ng)):
            rows = slice(s * R + h * Q, s * R + (h + 1) * Q)
            a = acc_s[rows, :] * w_a[rows, :] + acc_f[rows, :] * w_f[rows, :]
            high = a.astype(BF16)
            low = (a - high.astype(F32)).astype(BF16)
            both = jnp.dot(
                jnp.concatenate([high, low], axis=0), wv[s, h], preferred_element_type=F32
            )
            osend[s, :, h * vh:(h + 1) * vh] = both[:Q] + both[Q:]

    gcols = (hh // ng) * vh

    def cols_of(g):
        return pl.ds(g * gcols, gcols) if g < ng else pl.ds(hh * vh, 128)

    def ex_copy(s, g):
        return pltpu.make_async_remote_copy(
            src_ref=osend.at[s, :, cols_of(g)], dst_ref=orecv.at[facing[s], :, cols_of(g)],
            send_sem=ex_ss, recv_sem=ex_rs.at[facing[s] * (ng + 1) + g],
            device_id={"seq": other}, device_id_type=MESH,
        )

    s_f = lax.dot_general(
        qf[...], fx[...], (((1,), (1,)), ((), ())), preferred_element_type=F32
    )
    m_f = jnp.maximum(jnp.max(s_f, axis=1, keepdims=True), FLOOR)
    p_f = jnp.exp(s_f - m_f)
    l_f = jnp.sum(p_f, axis=1, keepdims=True)
    acc_f = jnp.dot(p_f.astype(BF16), fx[:, :rank], preferred_element_type=F32)
    m_own = jnp.maximum(m_a, m_f)
    w_a, w_f = jnp.exp(m_a - m_own), jnp.exp(m_f - m_own)

    def share(s):
        rows = slice(s * R, (s + 1) * R)
        l_own = jnp.sum(l_s[rows, :], axis=1, keepdims=True) * w_a[rows, :]
        l_own = l_own + l_f[rows, :] * w_f[rows, :]
        lane = lax.broadcasted_iota(jnp.int32, (Q, 128), 1)
        stats = jnp.zeros((Q, 128), F32)
        for h in range(hh):
            at = s * R + h * Q
            stats = jnp.where(lane == h, m_own[at:at + Q, :], stats)
            stats = jnp.where(lane == hh + h, l_own[h * Q:(h + 1) * Q, :], stats)
        osend[s, :, hh * vh:] = stats

    def expand(s, g):
        for h in range(g * (hh // ng), (g + 1) * (hh // ng)):
            rows = slice(s * R + h * Q, s * R + (h + 1) * Q)
            a = acc_s[rows, :] * w_a[rows, :] + acc_f[rows, :] * w_f[rows, :]
            high = a.astype(BF16)
            low = (a - high.astype(F32)).astype(BF16)
            both = jnp.dot(
                jnp.concatenate([high, low], axis=0), wv[s, h], preferred_element_type=F32
            )
            osend[s, :, h * vh:(h + 1) * vh] = both[:Q] + both[Q:]

    gcols = (hh // ng) * vh

    def cols_of(g):
        return pl.ds(g * gcols, gcols) if g < ng else pl.ds(hh * vh, 128)

    def ex_copy(s, g):
        return pltpu.make_async_remote_copy(
            src_ref=osend.at[s, :, cols_of(g)], dst_ref=orecv.at[facing[s], :, cols_of(g)],
            send_sem=ex_ss, recv_sem=ex_rs.at[facing[s] * (ng + 1) + g],
            device_id={"seq": other}, device_id_type=MESH,
        )

    def put(s, g):
        start = halves[s] * (hh * vh) + g * gcols
        if split:
            start = pl.multiple_of(start, 128)
        return pltpu.make_async_copy(
            att.at[s, :, cols_of(g)], att_hbm.at[:, pl.ds(start, gcols)], o_sem.at[s * ng + g]
        )

    finish(own, ne - 1)
    share(0)
    share(1)
    finish(theirs, ne - 1)
    for g in range(ng):
        expand(0, g)
    for s in range(2):
        ex_copy(s, ng).start()
    for g in range(ng):
        ex_copy(0, g).start()
    for g in range(ng):
        expand(1, g)
        ex_copy(1, g).start()

    for s in range(2):
        ex_copy(s, ng).wait_recv()
    weights = []
    for s in range(2):
        stats, others = osend[s, :, hh * vh:], orecv[s, :, hh * vh:]
        m_o, m_t = stats[:, :hh], others[:, :hh]
        joint = jnp.maximum(m_o, m_t)
        e_o, e_t = jnp.exp(m_o - joint), jnp.exp(m_t - joint)
        total = e_o * stats[:, hh:2 * hh] + e_t * others[:, hh:2 * hh]
        weights.append((e_o / total, e_t / total))
    for s in facing:
        e_o, e_t = weights[s]
        for g in range(ng):
            ex_copy(facing[s], g).wait_recv()
        for h in range(hh):
            cols = slice(h * vh, (h + 1) * vh)
            start = halves[s] * (hh * vh) + h * vh
            if split:
                start = pl.multiple_of(start, 128)
            att_ref[:, pl.ds(start, vh)] = (
                e_o[:, h:h + 1] * osend[s, :, cols] + e_t[:, h:h + 1] * orecv[s, :, cols]
            ).astype(BF16)

    settle(ql.at[pl.ds(0, T - 1)], ql_ss)
    settle(part.at[pl.ds(0, T - 1)], rs_ss)
    settle(rall.at[pl.ds(0, T - 1)], ag_ss)
    if split:
        for i in range(nq):
            qx_copy(i).wait_send()
    settle(osend, ex_ss)


def hand_over(reb_in, att_in, reb_out, att_out, sems):
    copies = [
        pltpu.make_async_copy(att_in, att_out, sems.at[0]),
        pltpu.make_async_copy(reb_in, reb_out, sems.at[1]),
    ]
    for c in copies:
        c.start()
    for c in copies:
        c.wait()


def body(
    stored_hidden, w_down_kv, kv_gain, evicted_blocks, query_latent, w_up_q,
    w_key_absorb, w_value, query_positions, prefix_lengths, latent_cache,
):
    T = lax.axis_size("tensor")
    rank = kv_gain.shape[0]
    heads, nope = w_key_absorb.shape[:2]
    width = w_down_kv.shape[1]
    rope_dim = width - rank
    Q = query_positions.shape[0]
    requests = prefix_lengths.shape[0]
    half_rows = stored_hidden.shape[1]
    local = half_rows // T
    cache_rows = latent_cache.shape[0]
    bk = min(2048, cache_rows)
    nb = cache_rows // bk
    kt = min(1024, cache_rows)
    ke = min(1024, cache_rows)
    kd = rank + -(-(rope_dim + requests) // 128) * 128
    head_qk = nope + rope_dim
    hh = heads // 2
    split = (hh * head_qk) % 128 == 0
    held = hh if split else heads
    nq = max(1, held // 4)
    ng = max(1, hh // 4)
    vh = w_value.shape[2]
    R = hh * Q
    half = np.arange(rope_dim // 2, dtype=np.float64) * (-2.0 / rope_dim)
    freq = jnp.asarray(np.tile(10000.0 ** half, 2)[None, :].astype(np.float32))
    cfg = (T, nope, rank, rope_dim, Q, requests, split, nq, nb, bk, ng, kt, ke)
    hbm = pl.BlockSpec(memory_space=pl.ANY)
    dma = pltpu.SemaphoreType.DMA
    pieces = 2 * (ng + 1)
    rebuilt = jax.ShapeDtypeStruct((1, local, width), BF16)
    attended = jax.ShapeDtypeStruct((Q, heads * vh), BF16)
    outs = pl.pallas_call(
        functools.partial(kernel, cfg),
        name="rebuild_attend",
        out_shape=(rebuilt, attended),
        in_specs=[hbm] * 12,
        out_specs=(pl.BlockSpec(memory_space=pltpu.VMEM),) * 2,
        scratch_shapes=[
            pltpu.SMEM(evicted_blocks.shape, jnp.int32),
            pltpu.SMEM(query_positions.shape, jnp.int32),
            pltpu.SMEM(prefix_lengths.shape, jnp.int32),
            pltpu.VMEM(freq.shape, F32),
            pltpu.VMEM(kv_gain.shape, BF16),
            pltpu.VMEM((half_rows, w_down_kv.shape[0]), BF16),
            pltpu.VMEM(w_down_kv.shape[::-1], BF16),
            pltpu.VMEM((T,) + query_latent.shape, BF16),
            pltpu.VMEM((Q, query_latent.shape[1]), F32),
            pltpu.VMEM((w_up_q.shape[0], held * head_qk), BF16),
            pltpu.VMEM((held,) + w_key_absorb.shape[1:], BF16),
            pltpu.VMEM((2, hh) + w_value.shape[1:], BF16),
            pltpu.VMEM((kd, cache_rows), BF16),
            pltpu.VMEM((2 * R, kd), BF16),
            pltpu.VMEM((T, local, width), F32),
            pltpu.VMEM((T, local, width), F32),
            pltpu.VMEM((local, width), BF16),
            pltpu.VMEM((T, local, width), BF16),
            pltpu.VMEM((half_rows, kd), BF16),
            pltpu.VMEM((2 * R, cache_rows), F32),
            pltpu.VMEM((2 * R, 1 * ke), BF16),
            pltpu.VMEM((2 * R, 128), F32),
            pltpu.VMEM((2 * R, 128), F32),
            pltpu.VMEM((2 * R, rank), F32),
            pltpu.VMEM((2, Q, hh * vh + 128), F32),
            pltpu.VMEM((2, Q, hh * vh + 128), F32),
            dma((5,)), dma((6,)), dma, dma, dma, dma, dma, dma, dma, dma,
            dma, dma((pieces,)), dma((nq,)), dma((nq,)),
        ],
        compiler_params=pltpu.CompilerParams(
            collective_id=0, has_side_effects=True, vmem_limit_bytes=52000 * 1024
        ),
    )(
        evicted_blocks,
        *(pltpu.with_memory_space_constraint(x, pltpu.HBM) for x in (
            query_positions, prefix_lengths, freq, kv_gain, stored_hidden, w_down_kv.T,
            query_latent, w_up_q, w_key_absorb, w_value, latent_cache.T,
        )),
    )
    return pl.pallas_call(
        hand_over,
        name="hand_over",
        out_shape=(rebuilt, attended),
        in_specs=[hbm] * 2,
        out_specs=(hbm,) * 2,
        scratch_shapes=[dma((2,))],
        compiler_params=pltpu.CompilerParams(vmem_limit_bytes=52000 * 1024),
    )(*outs)


def solution(mesh):
    placed = (
        P(("groups", "seq"), None, "tensor"),
        P("tensor", None),
        P(),
        P("groups"),
        P(("groups", "tensor"), None),
        P(None, "tensor"),
        P("tensor", None, None),
        P("tensor", None, None),
        P("groups"),
        P("groups"),
        P(("groups", "seq"), None),
    )
    return jax.shard_map(
        body,
        mesh=mesh,
        in_specs=placed,
        out_specs=(P(("groups", "seq"), "tensor", None), P("groups", "tensor")),
        check_vma=False,
    )
```
